512 devices in a mesh: tm: 64 (over y, z), plane: 8 (over x, core).
Axes of the slice: x: 4, y: 8, z: 8, core: 2. Of those that a mesh axis runs over, the one named last changes fastest.
Arguments:
- frames: bfloat16 [64, 16, 128, 1024], P('tm', 'plane'), may hold values from -6 to 6
- offsets: int32 [64, 16, 2], P('tm', 'plane'), may hold values from -64 to 64
- assign: int32 [64, 16, 1, 8, 1], P('tm', 'plane'), may hold values from 0 to 7; in each aligned block of 16 rows (0 to 15, 16 to 31, ..., all dimensions but the last counted through in order) at most 4 rows name the same one
- residual: int32 [64, 16, 1, 8, 2], P('tm', 'plane'), may hold values from -8 to 8
- template: bfloat16 [16, 128, 1024], P(None, None, 'plane'), may hold values from -6 to 6
Outputs:
- new_template: bfloat16 [16, 128, 1024], P(None, None, 'plane')
- scores: float32 [2, 64, 16, 1, 8], P(None, 'tm', 'plane')
The draws below stay inside these ranges and needn't reach their ends.
Inputs may be any that keep to these rules, and one draw needn't show every extreme that they name: `assign`: in each aligned block of 16 rows (the patches of one volume and one plane group), no column is named more than 4 times; one column is named exactly 4 times in some block.
All inputs are finite; a program needn't handle non-finite values.
Results may differ from the reference program's by a relative error of at most 0.004.
Values may be sent and summed in bfloat16 or wider, within the bound.
No kernel may reach another device: no remote copies, remote signals or barrier semaphores. Data moves between devices by JAX's collectives and lax.ppermute only.
A program may use at most 64 MiB of HBM per device.

```python
import math
import jax
import jax.numpy as jnp
import numpy as np
from jax import lax

PATCH = 128
GRID_R = 1
PLANE_DEV = 2
ROUNDS = 2
RES = 8
PLANES = 16
VOLS = 64
CAP = 4
N_PLANE = 8


def draw_frames(key, part):
    shape = (VOLS, PLANES, GRID_R * PATCH, N_PLANE * PATCH)
    noise_key = jax.random.fold_in(key, 11)
    pick_key = jax.random.fold_in(key, 12)
    level_key = jax.random.fold_in(key, 13)
    base = jnp.clip(jax.random.normal(noise_key, shape, jnp.float32), -6.0, 6.0)
    dimmed = jax.random.randint(pick_key, (VOLS,), 0, 2) == 1
    levels = jnp.exp(jax.random.uniform(level_key, (VOLS,), jnp.float32, math.log(0.01), math.log(0.05)))
    factor = jnp.where(dimmed, levels, jnp.ones((VOLS,), jnp.float32))
    return (base * factor[:, None, None, None]).astype(jnp.bfloat16)


def plant(result, key, low, largest):
    extent = result.shape
    spot = [jax.random.randint(jax.random.fold_in(key, axis), (), 0, extent[axis]) for axis in range(len(extent))]
    result = result.at[tuple(spot)].set(low)
    longest = extent.index(max(extent))
    spot[longest] = (spot[longest] + 1) % extent[longest]
    return result.at[tuple(spot)].set(largest)


def block_scale(own_key, shape, split, smallest, top_value):
    def one(axis_at, parts):
        heights = jax.random.uniform(jax.random.fold_in(jax.random.fold_in(own_key, 6), axis_at), (parts,), jnp.float32, smallest / len(split), top_value / len(split))
        return jnp.repeat(jnp.exp(heights), shape[axis_at] // parts).reshape((-1,) + (1,) * (len(shape) - axis_at - 1))

    factor_of = one(*split[0])
    for cut in split[1:]:
        factor_of = factor_of * one(*cut)
    return factor_of


def shared_out(rng, own, number, rows, count, top, most, slope):
    ranking = jax.random.permutation(rng, count)
    crowded, usual = portions_of(count, rows * top, most, slope, True), portions_of(count, rows * top, most, slope, False)
    places = jnp.arange(count)

    def named(sizes, offset_by):
        used = int((sizes > 0).sum())
        fixed = max(1, used // 4)
        passed = fixed + (places - fixed + offset_by * (used - fixed)) % max(1, count - fixed)
        return jnp.zeros((count,), jnp.int32).at[ranking[jnp.where(places < fixed, places, passed)]].set(jnp.asarray(sizes, jnp.int32))

    sizes = jnp.where(number % 4 == 0, named(crowded, number // 4), named(usual, number - number // 4 - 1))
    mixed = jax.random.permutation(jax.random.fold_in(own, 3), count)
    donor, sink = mixed[0:count // 2 * 2:2], mixed[1:count // 2 * 2:2]
    slack = jnp.minimum(sizes[donor] - 1, most - sizes[sink]) // 2
    slack = jnp.where((donor == ranking[0]) | (sink == ranking[0]) | (sizes[sink] == 0), 0, jnp.maximum(slack, 0))
    passed = jax.random.randint(jax.random.fold_in(own, 4), (count // 2,), 0, 1 << 20) % (slack + 1)
    sizes = sizes.at[donor].add(-passed).at[sink].add(passed)
    items = jnp.searchsorted(jnp.cumsum(sizes), jnp.arange(rows * top), side="right").astype(jnp.int32)
    listing = items.reshape(top, rows).T
    listing = listing[jax.random.permutation(jax.random.fold_in(own, 1), rows)]
    offset_by = jax.random.randint(jax.random.fold_in(own, 2), (rows, 1), 0, top)
    return jnp.take_along_axis(listing, (jnp.arange(top)[None, :] + offset_by) % top, axis=1)


def portions_of(count, total, limit, lean, full):
    portions = [(1 << 20) // math.isqrt(rank ** lean) + 1 for rank in range(1, count + 1)]
    largest = limit if full else min(limit, max(-(-total // count), total * portions[0] // sum(portions)))
    least = 1 if total - largest >= count - 1 else 0
    given, surplus = [largest] + [least] * (count - 1), total - largest - least * (count - 1)
    while surplus > 0:
        candidates = [i for i in range(1, count) if given[i] < largest] or [i for i in range(1, count) if given[i] < limit]
        mass, remaining = sum([portions[i] for i in candidates]), surplus
        for i in candidates:
            more = min(limit - given[i], max(1, remaining * portions[i] // mass), surplus)
            given[i] = given[i] + more
            surplus = surplus - more
    return np.array(given)


def centred(stream_key, dims, spread, most, pieces=(), kind=jnp.bfloat16):
    entries = spread * jax.random.normal(stream_key, dims, jnp.float32)
    if pieces:
        entries = entries * block_scale(stream_key, dims, pieces, -0.22, 0.18)
    return jnp.clip(entries, -most, most).astype(kind)


def setup_inputs(seed: int = 0) -> dict:
    key_list = jax.random.split(jax.random.key(seed), 6)
    frames = draw_frames(jax.random.fold_in(key_list[5], 71), 0)
    offsets = plant(jax.random.randint(key_list[1], (VOLS, PLANES, 2), -(PATCH // 2), PATCH // 2 + 1), jax.random.fold_in(key_list[1], 1), -(PATCH // 2), (PATCH // 2 + 1) - 1).astype(jnp.int32)
    assign_keys = jax.random.split(jax.random.fold_in(key_list[2], 1), VOLS * PLANES * GRID_R * N_PLANE // (PLANE_DEV * GRID_R * N_PLANE))
    assign_turns = jax.random.permutation(jax.random.fold_in(key_list[2], 3), VOLS * PLANES * GRID_R * N_PLANE // (PLANE_DEV * GRID_R * N_PLANE))
    assign = jax.vmap(lambda own, number: shared_out(jax.random.fold_in(key_list[2], 2), own, number, PLANE_DEV * GRID_R * N_PLANE, N_PLANE, 1, CAP, 2))(assign_keys, assign_turns).reshape((VOLS, PLANES, GRID_R, N_PLANE, 1))
    residual = plant(jax.random.randint(key_list[3], (VOLS, PLANES, GRID_R, N_PLANE, 2), -RES, RES + 1), jax.random.fold_in(key_list[3], 1), -RES, RES).astype(jnp.int32)
    template = centred(key_list[4], (PLANES, GRID_R * PATCH, N_PLANE * PATCH), 1.0, 6.0, ((2, 8),))
    return {"frames": frames, "offsets": offsets, "assign": assign, "residual": residual, "template": template}


highest = lax.Precision.HIGHEST

def dft_tables(length):
    indices = jnp.arange(length, dtype=jnp.int32)
    phases = (indices[:, None] * indices[None, :] % length).astype(jnp.float32) * (2.0 * math.pi / length)
    return (jnp.cos(phases).astype(jnp.bfloat16), jnp.sin(phases).astype(jnp.bfloat16))

def cyclic(source, amount, which_axis):
    length = source.shape[which_axis]
    doubled = jnp.concatenate([source, source], which_axis)
    return lax.dynamic_slice_in_dim(doubled, (amount % length).astype(jnp.int32), length, which_axis)

def shift_plane(frame_img, plane_off):
    return cyclic(cyclic(frame_img, plane_off[0], 0), plane_off[1], 1)

def to_tiles(tile_batch, patch_size):
    plane_count, tall, broad = tile_batch.shape
    shaped = tile_batch.reshape(plane_count, tall // patch_size, patch_size, broad // patch_size, patch_size)
    return shaped.transpose(0, 1, 3, 2, 4)

def from_tiles(tiled):
    plane_count, row_count, col_count, patch_size, patch_wide = tiled.shape
    return tiled.transpose(0, 1, 3, 2, 4).reshape(plane_count, row_count * patch_size, col_count * patch_wide)

def spectrum(tile_batch, cos_t, sin_t):
    values = tile_batch.astype(jnp.float32)
    cosine = cos_t.astype(jnp.float32)
    sine_table = sin_t.astype(jnp.float32)
    first_re = jnp.einsum('nyx,xk->nyk', values, cosine, precision=highest)
    first_im = -jnp.einsum('nyx,xk->nyk', values, sine_table, precision=highest)
    first_re = lax.optimization_barrier(first_re.astype(jnp.bfloat16)).astype(jnp.float32)
    first_im = lax.optimization_barrier(first_im.astype(jnp.bfloat16)).astype(jnp.float32)
    spec_re = jnp.einsum('uy,nyk->nuk', cosine, first_re, precision=highest) + jnp.einsum('uy,nyk->nuk', sine_table, first_im, precision=highest)
    spec_im = jnp.einsum('uy,nyk->nuk', cosine, first_im, precision=highest) - jnp.einsum('uy,nyk->nuk', sine_table, first_re, precision=highest)
    return (spec_re, spec_im)

def assess(patches, temp_re, temp_im, shift_rows, shift_cols, live_mask, cos_t, sin_t):
    patch_size = patches.shape[1]
    patch_re, patch_im = spectrum(patches, cos_t, sin_t)
    cross_re = patch_re * temp_re + patch_im * temp_im
    cross_im = patch_im * temp_re - patch_re * temp_im
    modulus = jnp.sqrt(cross_re * cross_re + cross_im * cross_im)
    levels = lax.optimization_barrier(jnp.mean(modulus, axis=(1, 2), keepdims=True))
    divisor = modulus + 0.1 * levels + 1e-06
    norm_re = lax.optimization_barrier((cross_re / divisor).astype(jnp.bfloat16)).astype(jnp.float32)
    norm_im = lax.optimization_barrier((cross_im / divisor).astype(jnp.bfloat16)).astype(jnp.float32)
    row_a = (shift_rows % patch_size).astype(jnp.int32)
    row_b = (shift_cols % patch_size).astype(jnp.int32)
    cos_a = cos_t[row_a].astype(jnp.float32)
    sin_a = sin_t[row_a].astype(jnp.float32)
    cos_b = cos_t[row_b].astype(jnp.float32)
    sin_b = sin_t[row_b].astype(jnp.float32)
    re_cos = jnp.einsum('nuv,nv->nu', norm_re, cos_b, precision=highest)
    re_sin = jnp.einsum('nuv,nv->nu', norm_re, sin_b, precision=highest)
    im_cos = jnp.einsum('nuv,nv->nu', norm_im, cos_b, precision=highest)
    im_sin = jnp.einsum('nuv,nv->nu', norm_im, sin_b, precision=highest)
    scores = (lax.optimization_barrier(jnp.sum(cos_a * re_cos, 1)) - lax.optimization_barrier(jnp.sum(sin_a * re_sin, 1)) - lax.optimization_barrier(jnp.sum(sin_a * im_cos, 1)) - lax.optimization_barrier(jnp.sum(cos_a * im_sin, 1))) / patch_size
    weights = (0.5 + jax.nn.sigmoid(scores)) * live_mask
    registered = jax.vmap(lambda single, shift_down, shift_across: cyclic(cyclic(single, shift_down, 0), shift_across, 1))(patches, shift_rows, shift_cols)
    contrib = registered.astype(jnp.float32) * weights[:, None, None]
    return (contrib, weights, scores)

def reference(frames, offsets, assign, residual, template):
    patch_size = PATCH
    rows_n = GRID_R
    cols_n = N_PLANE
    planes_n = PLANES
    cos_t, sin_t = dft_tables(patch_size)
    patch_count = planes_n * rows_n * cols_n
    plane_grid = jnp.arange(planes_n, dtype=jnp.int32)[:, None, None] * jnp.ones((1, rows_n, cols_n), jnp.int32)
    row_grid = jnp.arange(rows_n, dtype=jnp.int32)[None, :, None] * jnp.ones((planes_n, 1, cols_n), jnp.int32)
    base_index = ((plane_grid * rows_n + row_grid) * cols_n).reshape(patch_count)
    current = template
    score_list = []
    for round_index in range(ROUNDS):
        tile_stack = to_tiles(current, patch_size).reshape(patch_count, patch_size, patch_size)
        temp_re, temp_im = spectrum(tile_stack, cos_t, sin_t)

        def one_volume(carry, inputs):
            frame_img, offset_pair, owner_cols, shift_pairs = inputs
            shifted = jax.vmap(shift_plane)(frame_img, offset_pair)
            patches = to_tiles(shifted, patch_size).reshape(patch_count, patch_size, patch_size)
            target = base_index + owner_cols.reshape(patch_count).astype(jnp.int32)
            contrib, weights, scores = assess(patches, temp_re[target], temp_im[target], shift_pairs[..., 0].reshape(patch_count), shift_pairs[..., 1].reshape(patch_count), jnp.ones((patch_count,), jnp.float32), cos_t, sin_t)
            tile_sums, weight_sums = carry
            tile_sums = tile_sums.at[target].add(contrib)
            weight_sums = weight_sums.at[target].add(weights)
            return ((tile_sums, weight_sums), scores.reshape(planes_n, rows_n, cols_n))
        initial = (jnp.zeros((patch_count, patch_size, patch_size), jnp.float32), jnp.zeros((patch_count,), jnp.float32))
        (tile_sums, weight_sums), scores = lax.scan(one_volume, initial, (frames, offsets, assign, residual))
        renewed = ((tile_stack.astype(jnp.float32) + tile_sums) / (1.0 + weight_sums)[:, None, None]).astype(jnp.bfloat16)
        current = from_tiles(renewed.reshape(planes_n, rows_n, cols_n, patch_size, patch_size))
        score_list.append(scores)
    return (current, jnp.stack(score_list))
```

```python
import functools

import jax
import jax.numpy as jnp
import numpy as np
from jax import lax
from jax.experimental import pallas as pl
from jax.experimental.pallas import tpu as pltpu
from jax.sharding import PartitionSpec as P

N = 128
COLS = 8
PD = 2
K = PD * COLS
TM = 64
SL = TM // PD
RR = N // SL
W = RR * N
F32, BF16 = jnp.float32, jnp.bfloat16


def tables():
    j = np.arange(N, dtype=np.int32)
    phase = (j[:, None] * j[None, :] % N).astype(np.float32) * np.float32(2.0 * np.pi / N)
    cos = np.cos(phase).astype(BF16)
    sin = np.sin(phase).astype(BF16)
    right = np.concatenate([cos, -sin], 1)
    left = np.concatenate(
        [np.concatenate([cos, sin], 1), np.concatenate([-sin, cos], 1)], 0
    )
    rows = np.concatenate([cos, sin], 1).astype(np.float32)
    return right, left, rows


def transform_pair(pair, right, left):
    first = jnp.dot(pair, right, preferred_element_type=F32).astype(BF16)
    inner = jnp.concatenate(
        [
            jnp.concatenate([first[:N, :N], first[N:, :N]], 1),
            jnp.concatenate([first[:N, N:], first[N:, N:]], 1),
        ],
        0,
    )
    return jnp.dot(left, inner, preferred_element_type=F32)


def prep_kernel(off, res, frames, right, left, spec, reg_out, shifted, regs):
    for p in range(PD):
        plane = frames[p].astype(F32)
        plane = pltpu.roll(plane, (-off[p, 0]) & (N - 1), 0)
        plane = pltpu.roll(plane, (-off[p, 1]) & (COLS * N - 1), 1)
        shifted[p] = plane
    for p in range(PD):
        for c in range(0, COLS, 2):
            k = p * COLS + c
            one = shifted[p, :, c * N : (c + 1) * N]
            two = shifted[p, :, (c + 1) * N : (c + 2) * N]
            pair = jnp.concatenate([one, two], 0).astype(BF16)
            both = transform_pair(pair, right[...], left[...])
            spec[k] = both[:, :N]
            spec[k + 1] = both[:, N:]
            for d, patch in ((0, one), (1, two)):
                moved = pltpu.roll(patch, (-res[k + d, 0]) & (N - 1), 0)
                regs[p, c + d] = pltpu.roll(moved, (-res[k + d, 1]) & (N - 1), 1)
        for r in range(RR):
            block = regs[p, :, r * SL : (r + 1) * SL, :]
            block = jnp.transpose(block, (1, 0, 2))
            reg_out[p * SL : (p + 1) * SL, :, r * N : (r + 1) * N] = block.astype(BF16)


def score_patches(asg, res, rows, spec, tspec, srow):
    def one(k, carry):
        tile = (k // COLS) * COLS + asg[k]
        p_re, p_im = spec[k, :N, :], spec[k, N:, :]
        t_re, t_im = tspec[tile, :N, :], tspec[tile, N:, :]
        c_re = p_re * t_re + p_im * t_im
        c_im = p_im * t_re - p_re * t_im
        modulus = jnp.sqrt(c_re * c_re + c_im * c_im)
        level = jnp.sum(jnp.sum(modulus, 0, keepdims=True), 1, keepdims=True) * (1.0 / (N * N))
        scale = 1.0 / (modulus + 0.1 * level + 1e-06)
        n_re = (c_re * scale).astype(BF16)
        n_im = (c_im * scale).astype(BF16)
        row_a = rows[pl.ds(res[k, 0] & (N - 1), 1), :]
        row_b = rows[pl.ds(res[k, 1] & (N - 1), 1), :]
        lhs = jnp.concatenate([row_a[:, :N], row_a[:, N:]], 0).astype(BF16)
        s_re = jnp.dot(lhs, n_re, preferred_element_type=F32)
        s_im = jnp.dot(lhs, n_im, preferred_element_type=F32)
        along = row_b[:, :N] * (s_re[0:1] - s_im[1:2]) - row_b[:, N:] * (s_re[1:2] + s_im[0:1])
        srow[pl.ds(k, 1), :] = along
        return carry

    lax.fori_loop(0, K, one, 0, unroll=2)
    return jnp.sum(srow[...], 1, keepdims=True) * (1.0 / N)


def pieces(value):
    high = value.astype(BF16).astype(F32)
    rest = value - high
    mid = rest.astype(BF16).astype(F32)
    return high, mid, rest - mid


def first_kernel(ids, asg, res, asg_col, temp, spec, reg_in, right, left, rows, msg, score_out, slab, tspec, srow, wide):
    for c in range(COLS):
        both = transform_pair(temp[c], right[...], left[...])
        tspec[c] = both[:, :N]
        tspec[COLS + c] = both[:, N:]
    for c in range(COLS):
        wide[...] = temp[c].astype(F32)
        for r in range(RR):
            slab[c : c + 1, r * N : (r + 1) * N] = wide[pl.ds(ids[0] * N + r * SL + ids[1], 1), :]
    score = score_patches(asg, res, rows, spec, tspec, srow)
    weight = 0.5 + 1.0 / (1.0 + jnp.exp(-score))
    high, mid, low = pieces(weight)
    lane = lax.broadcasted_iota(jnp.int32, (K, N), 1)
    col = asg_col[...]
    meta = jnp.where(lane == 32, 1.0, 0.0)
    meta = jnp.where(lane == col, high, meta)
    meta = jnp.where(lane == col + 8, mid, meta)
    meta = jnp.where(lane == col + 16, low, meta).astype(BF16)
    msg[:, :, :W] = reg_in[...]
    for p in range(PD):
        msg[p * SL : (p + 1) * SL, :, W:] = jnp.broadcast_to(
            meta[p * COLS : (p + 1) * COLS][None], (SL, COLS, N)
        )
    score_out[...] = jnp.broadcast_to(score, (K, N))


def renew_kernel(got, old, new, msg):
    out = lax.dot_general(
        got[:, W:], got[...], (((0,), (0,)), ((), ())), preferred_element_type=F32
    )
    total = out[0:8] + out[8:16] + out[16:24]
    fresh = (old[...] + total[:, :W]) / (1.0 + total[:, W + 32 : W + 33])
    fresh = fresh.astype(BF16)
    new[...] = fresh.astype(F32)
    msg[...] = jnp.broadcast_to(fresh[None], (TM, COLS, W))


def second_kernel(asg, res, asg_col, got, spec, right, left, rows, msg, score_out, tspec, srow, tiles):
    for p in range(PD):
        for r in range(RR):
            block = got[p * SL : (p + 1) * SL, :, r * N : (r + 1) * N].astype(F32)
            block = jnp.transpose(block, (1, 0, 2))
            tiles[:, p * N + r * SL : p * N + (r + 1) * SL, :] = block.astype(BF16)
    for c in range(COLS):
        both = transform_pair(tiles[c], right[...], left[...])
        tspec[c] = both[:, :N]
        tspec[COLS + c] = both[:, N:]
    score = score_patches(asg, res, rows, spec, tspec, srow)
    weight = 0.5 + 1.0 / (1.0 + jnp.exp(-score))
    lane = lax.broadcasted_iota(jnp.int32, (K, N), 1)
    at = lax.broadcasted_iota(jnp.int32, (K, N), 0) * COLS + asg_col[...]
    row = jnp.sum(jnp.where(lane == at, weight, 0.0), 0, keepdims=True)
    msg[...] = jnp.broadcast_to(row[None], (TM, 1, N))
    score_out[...] = jnp.broadcast_to(score, (K, N))


def last_kernel(ids, got, got_w, old, fin):
    count = TM * COLS
    row = lax.broadcasted_iota(jnp.int32, (count, N), 0)
    lane = lax.broadcasted_iota(jnp.int32, (count, N), 1)
    keep = (lane // COLS) == (row % COLS) + ids[0] * COLS
    pick = lax.broadcasted_iota(jnp.int32, (count, TM), 0) // COLS
    pick = (pick == lax.broadcasted_iota(jnp.int32, (count, TM), 1)).astype(BF16)
    out = jnp.zeros((N, W + N), F32)
    for piece in pieces(got_w[...]):
        part = jnp.dot(pick, piece.astype(BF16), preferred_element_type=F32)
        part = jnp.where(keep, part, 0.0).astype(BF16)
        out = out + lax.dot_general(
            part, got[...], (((0,), (0,)), ((), ())), preferred_element_type=F32
        )
    total = out[0:COLS]
    for m in range(1, N // COLS):
        total = total + out[m * COLS : (m + 1) * COLS]
    fresh = (old[...] + total[:, :W]) / (1.0 + total[:, W + 32 : W + 33])
    for c in range(COLS):
        parts = [fresh[c : c + 1, r * N : (r + 1) * N] for r in range(RR)]
        fin[c] = jnp.concatenate(parts, 0).astype(BF16)


def place_kernel(got, out):
    for p in range(PD):
        for g in range(COLS):
            block = got[p * SL : (p + 1) * SL, g * RR : (g + 1) * RR, :].astype(F32)
            block = jnp.transpose(block, (1, 0, 2)).reshape(N, N)
            out[PD * g + p] = block.astype(BF16)


def call(kernel, name, outs, ins, scratch, args, flops=1e8):
    spaces = {"s": pltpu.SMEM, "v": pltpu.VMEM}
    size = sum(int(np.prod(o.shape)) * o.dtype.itemsize for o in outs)
    return pl.pallas_call(
        kernel,
        name=name,
        out_shape=outs,
        in_specs=[pl.BlockSpec(memory_space=spaces[i]) for i in ins],
        out_specs=[pl.BlockSpec(memory_space=pltpu.VMEM) for _ in outs],
        scratch_shapes=scratch,
        compiler_params=pltpu.CompilerParams(vmem_limit_bytes=40 << 20),
        cost_estimate=pl.CostEstimate(flops=int(flops), bytes_accessed=size + (1 << 20), transcendentals=0),
    )(*args)


def struct(shape, dtype):
    return jax.ShapeDtypeStruct(shape, dtype)


def local(frames, offsets, assign, residual, template):
    right, left, rows = (jnp.asarray(t) for t in tables())
    off = offsets.reshape(PD, 2)
    asg = assign.reshape(K)
    res = residual.reshape(K, 2)
    col = assign.reshape(K, 1)
    t = lax.axis_index("tm").astype(jnp.int32)
    ids = jnp.stack([t // SL, t % SL])
    spec_shape = (K, 2 * N, N)
    temp = lax.all_to_all(
        template.reshape(COLS, PD * N, N), "plane", split_axis=0, concat_axis=0, tiled=True
    )
    spec, reg = call(
        prep_kernel,
        "prep",
        [struct(spec_shape, F32), struct((TM, COLS, W), BF16)],
        "ssvvv",
        [pltpu.VMEM((PD, N, COLS * N), F32), pltpu.VMEM((PD, COLS, N, N), F32)],
        (off, res, frames[0], right, left),
        flops=4e8,
    )
    msg, score_a, slab = call(
        first_kernel,
        "first",
        [struct((TM, COLS, W + N), BF16), struct((K, N), F32), struct((COLS, W), F32)],
        "sssvvvvvvv",
        [pltpu.VMEM(spec_shape, F32), pltpu.VMEM((K, N), F32), pltpu.VMEM((2 * N, N), F32)],
        (ids, asg, res, col, temp, spec, reg, right, left, rows),
        flops=4e8,
    )
    got = lax.all_to_all(
        msg.reshape(TM * COLS, W + N), "tm", split_axis=0, concat_axis=0, tiled=True
    )
    slab, msg = call(
        renew_kernel,
        "renew",
        [struct((COLS, W), F32), struct((TM, COLS, W), BF16)],
        "vv",
        [],
        (got, slab),
    )
    tiles = lax.all_to_all(msg, "tm", split_axis=0, concat_axis=0, tiled=True)
    msg, score_b = call(
        second_kernel,
        "second",
        [struct((TM, 1, N), F32), struct((K, N), F32)],
        "ssvvvvvv",
        [
            pltpu.VMEM(spec_shape, F32),
            pltpu.VMEM((K, N), F32),
            pltpu.VMEM((COLS, PD * N, N), BF16),
        ],
        (asg, res, col, tiles, spec, right, left, rows),
        flops=4e8,
    )
    got_w = lax.all_to_all(msg, "tm", split_axis=0, concat_axis=0, tiled=True).reshape(TM, N)
    (fin,) = call(
        last_kernel, "last", [struct((COLS, RR, N), BF16)], "svvv", [], (ids, got, got_w, slab)
    )
    fin = lax.all_to_all(fin, "plane", split_axis=0, concat_axis=0, tiled=True)
    msg = jnp.broadcast_to(fin.reshape(1, COLS * RR, N), (TM, COLS * RR, N))
    fin = lax.all_to_all(msg, "tm", split_axis=0, concat_axis=0, tiled=True)
    (out,) = call(place_kernel, "place", [struct((PD * COLS, N, N), BF16)], "v", [], (fin,))
    scores = jnp.stack([score_a[:, 0], score_b[:, 0]]).reshape(2, 1, PD, 1, COLS)
    return out, scores


def solution(mesh):
    return jax.shard_map(
        local,
        mesh=mesh,
        in_specs=(
            P("tm", "plane", None, None),
            P("tm", "plane", None),
            P("tm", "plane", None, None, None),
            P("tm", "plane", None, None, None),
            P(None, None, "plane"),
        ),
        out_specs=(P(None, None, "plane"), P(None, "tm", "plane", None, None)),
        check_vma=False,
    )
```

```python
import jax
import jax.numpy as jnp
import numpy as np
from jax import lax
from jax.experimental import pallas as pl
from jax.experimental.pallas import tpu as pltpu
from jax.sharding import PartitionSpec as P

N = 128
COLS = 8
PD = 2
K = PD * COLS
TM = 64
SL = TM // PD
RR = N // SL
W = RR * N
F32, BF16 = jnp.float32, jnp.bfloat16


def tables():
    j = np.arange(N, dtype=np.int32)
    phase = (j[:, None] * j[None, :] % N).astype(np.float32) * np.float32(2.0 * np.pi / N)
    cos = np.cos(phase).astype(BF16)
    sin = np.sin(phase).astype(BF16)
    right = np.concatenate([cos, -sin], 1)
    left = np.concatenate(
        [np.concatenate([cos, sin], 1), np.concatenate([-sin, cos], 1)], 0
    )
    rows = np.concatenate([cos, sin], 1).astype(np.float32)
    return right, left, rows


def transform_pair(pair, right, left):
    first = jnp.dot(pair, right, preferred_element_type=F32).astype(BF16)
    inner = jnp.concatenate(
        [
            jnp.concatenate([first[:N, :N], first[N:, :N]], 1),
            jnp.concatenate([first[:N, N:], first[N:, N:]], 1),
        ],
        0,
    )
    return jnp.dot(left, inner, preferred_element_type=F32)


def prep_kernel(off, res, frames, right, left, spec, reg_out, shifted, regs):
    for p in range(PD):
        plane = frames[p].astype(F32)
        plane = pltpu.roll(plane, (-off[p, 0]) & (N - 1), 0)
        plane = pltpu.roll(plane, (-off[p, 1]) & (COLS * N - 1), 1)
        shifted[p] = plane
    for p in range(PD):
        for c in range(0, COLS, 2):
            k = p * COLS + c
            one = shifted[p, :, c * N : (c + 1) * N]
            two = shifted[p, :, (c + 1) * N : (c + 2) * N]
            pair = jnp.concatenate([one, two], 0).astype(BF16)
            both = transform_pair(pair, right[...], left[...])
            spec[k] = both[:, :N]
            spec[k + 1] = both[:, N:]
            for d, patch in ((0, one), (1, two)):
                moved = pltpu.roll(patch, (-res[p, 0, c + d]) & (N - 1), 0)
                regs[p, c + d] = pltpu.roll(moved, (-res[p, 1, c + d]) & (N - 1), 1)
        for r in range(RR):
            block = regs[p, :, r * SL : (r + 1) * SL, :]
            block = jnp.transpose(block, (1, 0, 2))
            reg_out[p * SL : (p + 1) * SL, :, r * N : (r + 1) * N] = block.astype(BF16)


def score_patches(asg, res, rows, spec, tspec, srow):
    def one(k, carry):
        p, c = k // COLS, k % COLS
        tile = p * COLS + asg[p, c]
        p_re, p_im = spec[k, :N, :], spec[k, N:, :]
        t_re, t_im = tspec[tile, :N, :], tspec[tile, N:, :]
        c_re = p_re * t_re + p_im * t_im
        c_im = p_im * t_re - p_re * t_im
        modulus = jnp.sqrt(c_re * c_re + c_im * c_im)
        level = jnp.sum(jnp.sum(modulus, 0, keepdims=True), 1, keepdims=True) * (1.0 / (N * N))
        scale = 1.0 / (modulus + 0.1 * level + 1e-06)
        n_re = (c_re * scale).astype(BF16)
        n_im = (c_im * scale).astype(BF16)
        row_a = rows[pl.ds(res[p, 0, c] & (N - 1), 1), :]
        row_b = rows[pl.ds(res[p, 1, c] & (N - 1), 1), :]
        lhs = jnp.concatenate([row_a[:, :N], row_a[:, N:]], 0).astype(BF16)
        s_re = jnp.dot(lhs, n_re, preferred_element_type=F32)
        s_im = jnp.dot(lhs, n_im, preferred_element_type=F32)
        along = row_b[:, :N] * (s_re[0:1] - s_im[1:2]) - row_b[:, N:] * (s_re[1:2] + s_im[0:1])
        srow[pl.ds(k, 1), :] = along
        return carry

    lax.fori_loop(0, K, one, 0, unroll=8)
    return jnp.sum(srow[...], 1, keepdims=True) * (1.0 / N)


def column_of(asg):
    row = lax.broadcasted_iota(jnp.int32, (K, 1), 0)
    col = jnp.zeros((K, 1), jnp.int32)
    for k in range(K):
        col = jnp.where(row == k, asg[k // COLS, k % COLS], col)
    return col


def pieces(value):
    high = value.astype(BF16).astype(F32)
    rest = value - high
    mid = rest.astype(BF16).astype(F32)
    return high, mid, rest - mid


def first_kernel(ids, asg, res, temp, spec, reg_in, right, left, rows, msg, score_out, slab, tspec, srow, wide):
    for c in range(COLS):
        both = transform_pair(temp[c], right[...], left[...])
        tspec[c] = both[:, :N]
        tspec[COLS + c] = both[:, N:]
    for c in range(COLS):
        wide[...] = temp[c].astype(F32)
        for r in range(RR):
            slab[c : c + 1, r * N : (r + 1) * N] = wide[pl.ds(ids[0] * N + r * SL + ids[1], 1), :]
    score = score_patches(asg, res, rows, spec, tspec, srow)
    weight = 0.5 + 1.0 / (1.0 + jnp.exp(-score))
    high, mid, low = pieces(weight)
    lane = lax.broadcasted_iota(jnp.int32, (K, N), 1)
    col = column_of(asg)
    meta = jnp.where(lane == 32, 1.0, 0.0)
    meta = jnp.where(lane == col, high, meta)
    meta = jnp.where(lane == col + 8, mid, meta)
    meta = jnp.where(lane == col + 16, low, meta).astype(BF16)
    msg[:, :, :W] = reg_in[...]
    for p in range(PD):
        msg[p * SL : (p + 1) * SL, :, W:] = jnp.broadcast_to(
            meta[p * COLS : (p + 1) * COLS][None], (SL, COLS, N)
        )
    score_out[...] = jnp.broadcast_to(score, (K, N))


def renew_kernel(got, old, new, msg):
    out = lax.dot_general(
        got[:, W:], got[...], (((0,), (0,)), ((), ())), preferred_element_type=F32
    )
    total = out[0:8] + out[8:16] + out[16:24]
    fresh = (old[...] + total[:, :W]) / (1.0 + total[:, W + 32 : W + 33])
    fresh = fresh.astype(BF16)
    new[...] = fresh.astype(F32)
    msg[...] = jnp.broadcast_to(fresh[None], (TM, COLS, W))


def second_kernel(asg, res, got, spec, right, left, rows, msg, score_out, tspec, srow, tiles):
    for p in range(PD):
        for r in range(RR):
            block = got[p * SL : (p + 1) * SL, :, r * N : (r + 1) * N].astype(F32)
            block = jnp.transpose(block, (1, 0, 2))
            tiles[:, p * N + r * SL : p * N + (r + 1) * SL, :] = block.astype(BF16)
    for c in range(COLS):
        both = transform_pair(tiles[c], right[...], left[...])
        tspec[c] = both[:, :N]
        tspec[COLS + c] = both[:, N:]
    score = score_patches(asg, res, rows, spec, tspec, srow)
    weight = 0.5 + 1.0 / (1.0 + jnp.exp(-score))
    lane = lax.broadcasted_iota(jnp.int32, (K, N), 1)
    at = lax.broadcasted_iota(jnp.int32, (K, N), 0) * COLS + column_of(asg)
    row = jnp.sum(jnp.where(lane == at, weight, 0.0), 0, keepdims=True)
    msg[...] = jnp.broadcast_to(row[None], (TM, 1, N))
    score_out[...] = jnp.broadcast_to(score, (K, N))


def last_kernel(ids, got, got_w, old, fin):
    count = TM * COLS
    row = lax.broadcasted_iota(jnp.int32, (N, count), 0)
    lane = lax.broadcasted_iota(jnp.int32, (N, count), 1)
    keep = row // COLS == (lane & (COLS - 1)) + ids[0] * COLS
    pick = lax.broadcasted_iota(jnp.int32, (TM, count), 1) // COLS
    pick = (pick == lax.broadcasted_iota(jnp.int32, (TM, count), 0)).astype(BF16)
    total = jnp.zeros((COLS, W + N), F32)
    for piece in pieces(got_w[...]):
        part = lax.dot_general(
            piece.astype(BF16), pick, (((0,), (0,)), ((), ())), preferred_element_type=F32
        )
        part = jnp.where(keep, part, 0.0)
        spread = part[0:COLS]
        for m in range(1, N // COLS):
            spread = spread + part[m * COLS : (m + 1) * COLS]
        total = total + jnp.dot(spread.astype(BF16), got[...], preferred_element_type=F32)
    fresh = (old[...] + total[:, :W]) / (1.0 + total[:, W + 32 : W + 33])
    for c in range(COLS):
        parts = [fresh[c : c + 1, r * N : (r + 1) * N] for r in range(RR)]
        tile = jnp.concatenate(parts, 0).astype(BF16)
        fin[:, c] = jnp.broadcast_to(tile[None], (TM, RR, N))


def place_kernel(got, out):
    for p in range(PD):
        for g in range(COLS):
            block = got[p * SL : (p + 1) * SL, g].astype(F32)
            block = jnp.transpose(block, (1, 0, 2)).reshape(N, N)
            out[PD * g + p] = block.astype(BF16)


def call(kernel, name, outs, ins, scratch, args, flops=1e8):
    spaces = {"s": pltpu.SMEM, "v": pltpu.VMEM}
    size = sum(int(np.prod(o.shape)) * o.dtype.itemsize for o in outs)
    return pl.pallas_call(
        kernel,
        name=name,
        out_shape=outs,
        in_specs=[pl.BlockSpec(memory_space=spaces[i]) for i in ins],
        out_specs=[pl.BlockSpec(memory_space=pltpu.VMEM) for _ in outs],
        scratch_shapes=scratch,
        compiler_params=pltpu.CompilerParams(vmem_limit_bytes=40 << 20),
        cost_estimate=pl.CostEstimate(flops=int(flops), bytes_accessed=size + (1 << 20), transcendentals=0),
    )(*args)


def struct(shape, dtype):
    return jax.ShapeDtypeStruct(shape, dtype)


def local(frames, offsets, assign, residual, template):
    right, left, rows = (jnp.asarray(t) for t in tables())
    off = offsets.reshape(PD, 2)
    asg = assign.reshape(PD, COLS)
    res = residual.reshape(PD, COLS, 2).transpose(0, 2, 1)
    t = lax.axis_index("tm").astype(jnp.int32)
    ids = jnp.stack([t // SL, t % SL])
    spec_shape = (K, 2 * N, N)
    temp = lax.all_to_all(
        template.reshape(COLS, PD * N, N), "plane", split_axis=0, concat_axis=0, tiled=True
    )
    spec, reg = call(
        prep_kernel,
        "prep",
        [struct(spec_shape, F32), struct((TM, COLS, W), BF16)],
        "ssvvv",
        [pltpu.VMEM((PD, N, COLS * N), F32), pltpu.VMEM((PD, COLS, N, N), F32)],
        (off, res, frames[0], right, left),
        flops=4e8,
    )
    msg, score_a, slab = call(
        first_kernel,
        "first",
        [struct((TM, COLS, W + N), BF16), struct((K, N), F32), struct((COLS, W), F32)],
        "sssvvvvvv",
        [pltpu.VMEM(spec_shape, F32), pltpu.VMEM((K, N), F32), pltpu.VMEM((2 * N, N), F32)],
        (ids, asg, res, temp, spec, reg, right, left, rows),
        flops=4e8,
    )
    got = lax.all_to_all(
        msg.reshape(TM * COLS, W + N), "tm", split_axis=0, concat_axis=0, tiled=True
    )
    slab, msg = call(
        renew_kernel,
        "renew",
        [struct((COLS, W), F32), struct((TM, COLS, W), BF16)],
        "vv",
        [],
        (got, slab),
    )
    tiles = lax.all_to_all(msg, "tm", split_axis=0, concat_axis=0, tiled=True)
    msg, score_b = call(
        second_kernel,
        "second",
        [struct((TM, 1, N), F32), struct((K, N), F32)],
        "ssvvvvv",
        [
            pltpu.VMEM(spec_shape, F32),
            pltpu.VMEM((K, N), F32),
            pltpu.VMEM((COLS, PD * N, N), BF16),
        ],
        (asg, res, tiles, spec, right, left, rows),
        flops=4e8,
    )
    got_w = lax.all_to_all(msg, "tm", split_axis=0, concat_axis=0, tiled=True).reshape(TM, N)
    (fin,) = call(
        last_kernel, "last", [struct((TM, COLS, RR, N), BF16)], "svvv", [], (ids, got, got_w, slab)
    )
    fin = lax.all_to_all(
        fin.reshape(TM * COLS, RR, N), ("tm", "plane"), split_axis=0, concat_axis=0, tiled=True
    ).reshape(TM, COLS, RR, N)
    (out,) = call(place_kernel, "place", [struct((PD * COLS, N, N), BF16)], "v", [], (fin,))
    scores = jnp.stack([score_a[:, 0], score_b[:, 0]]).reshape(2, 1, PD, 1, COLS)
    return out, scores


def solution(mesh):
    return jax.shard_map(
        local,
        mesh=mesh,
        in_specs=(
            P("tm", "plane", None, None),
            P("tm", "plane", None),
            P("tm", "plane", None, None, None),
            P("tm", "plane", None, None, None),
            P(None, None, "plane"),
        ),
        out_specs=(P(None, None, "plane"), P(None, "tm", "plane", None, None)),
        check_vma=False,
    )
```

```python
import jax
import jax.numpy as jnp
import numpy as np
from jax import lax
from jax.experimental import pallas as pl
from jax.experimental.pallas import tpu as pltpu
from jax.sharding import PartitionSpec as P


N = 128
C = 8
PD = 2
CAP = 4
PAIRS = C * CAP // 2
ROWS = CAP * N + 16
SLAB = N // C
F32, BF16, I32 = jnp.float32, jnp.bfloat16, jnp.int32


def tables():
    j = np.arange(N, dtype=np.int32)
    phase = (j[:, None] * j[None, :] % N).astype(np.float32) * np.float32(2.0 * np.pi / N)
    cos = np.cos(phase).astype(BF16)
    sin = np.sin(phase).astype(BF16)
    right = np.concatenate([cos, -sin], 1)
    left = np.concatenate(
        [np.concatenate([cos, sin], 1), np.concatenate([-sin, cos], 1)], 0
    )
    rows = np.concatenate([cos, sin], 1)
    return right, left, rows


def dot(a, b):
    return jnp.dot(a, b, preferred_element_type=F32)


def transform_pair(pair, right, left):
    first = dot(pair, right).astype(BF16)
    inner = jnp.concatenate(
        [
            jnp.concatenate([first[:N, :N], first[N:, :N]], 1),
            jnp.concatenate([first[:N, N:], first[N:, N:]], 1),
        ],
        0,
    )
    return dot(left, inner)


def pieces(value):
    high = value.astype(BF16).astype(F32)
    rest = value - high
    mid = rest.astype(BF16).astype(F32)
    return high, mid, rest - mid


def iota(shape, axis):
    return lax.broadcasted_iota(I32, shape, axis)


def deal_kernel(off, asg, res, frames, out, shifted, details, count):
    out[...] = jnp.zeros_like(out)
    details[...] = jnp.zeros_like(details)
    for c in range(C):
        count[c] = 0
    for p in range(PD):
        plane = frames[p].astype(F32)
        plane = pltpu.roll(plane, (-off[p, 0]) & (N - 1), 0)
        plane = pltpu.roll(plane, (-off[p, 1]) & (C * N - 1), 1)
        shifted[p] = plane.astype(BF16)
    lane, row = iota((8, N), 1), iota((8, N), 0)
    for p in range(PD):
        for k in range(C):
            c = asg[p, k]
            slot = count[c]
            count[c] = slot + 1
            at = pl.multiple_of(slot * N, N)
            out[c, pl.ds(at, N), :] = shifted[p, :, k * N : (k + 1) * N]
            text = jnp.where(lane == 0, p, 0)
            text = jnp.where(lane == 1, res[p, 0, k], text)
            text = jnp.where(lane == 2, res[p, 1, k], text)
            text = jnp.where(lane == 3, 1, text)
            text = jnp.where(lane == 4, p * C + k, text).astype(F32)
            at = c * (CAP // 2) + slot // 2
            details[at] = jnp.where((row & 1) == (slot & 1), text, details[at])
    for c in range(C):
        for j in range(CAP // 2):
            out[c, CAP * N + 8 * j : CAP * N + 8 * (j + 1), :] = details[
                c * (CAP // 2) + j
            ].astype(BF16)


def tile_kernel(pair, right, left, spec):
    spec[...] = transform_pair(pair[...], right[...], left[...])


def along_of(both, tiles, info, phase):
    outs = []
    for e in range(2):
        p_re, p_im = both[:N, e * N : (e + 1) * N], both[N:, e * N : (e + 1) * N]
        upper = info[e : e + 1, 0:1] > 0.5
        t_re = jnp.where(upper, tiles[:N, N:], tiles[:N, :N])
        t_im = jnp.where(upper, tiles[N:, N:], tiles[N:, :N])
        c_re = p_re * t_re + p_im * t_im
        c_im = p_im * t_re - p_re * t_im
        modulus = jnp.sqrt(c_re * c_re + c_im * c_im)
        level = jnp.sum(jnp.sum(modulus, 0, keepdims=True), 1, keepdims=True) * (1.0 / (N * N))
        scale = 1.0 / (modulus + 0.1 * level + 1e-06)
        n_re = (c_re * scale).astype(BF16)
        n_im = (c_im * scale).astype(BF16)
        lhs = jnp.concatenate([phase[e : e + 1], phase[2 + e : 3 + e]], 0).astype(BF16)
        s_re, s_im = dot(lhs, n_re), dot(lhs, n_im)
        outs.append(
            phase[4 + e : 5 + e] * (s_re[0:1] - s_im[1:2])
            - phase[6 + e : 7 + e] * (s_re[1:2] + s_im[0:1])
        )
    return jnp.concatenate(outs, 0)


def match(spec, tiles, info, phase, along):
    along[...] = jnp.zeros_like(along)

    def one(i, carry):
        along[i, 0:2, :] = along_of(spec[i], tiles[...], info[i], phase[i])
        return carry

    lax.fori_loop(0, PAIRS, one, 0, unroll=8)


def weigh(along, info, w_low, w_high, turn):
    flat = info[...].reshape(C * 16, N)
    row = iota((C * 16, 1), 0)
    live = jnp.where((row & 7) < 2, flat[:, 3:4], 0.0)
    score = jnp.sum(along[...].reshape(C * 16, N), 1, keepdims=True) * (1.0 / N)
    weight = (0.5 + 1.0 / (1.0 + jnp.exp(-score))) * live
    high = weight * flat[:, 0:1]
    low = weight - high
    w_low[...] = jnp.broadcast_to(low, (C * 16, N)).reshape(PAIRS, 8, N)
    w_high[...] = jnp.broadcast_to(high, (C * 16, N)).reshape(PAIRS, 8, N)
    lane = iota((C * 16, N), 1)
    at = flat[:, 4:5].astype(I32) + turn * 16
    table = jnp.where(lane == at, score * live, 0.0).reshape(C, 16, N)
    return jnp.sum(table, 1), jnp.sum(low, 0, keepdims=True), jnp.sum(high, 0, keepdims=True)


def weighted(moved, w_low, w_high, low, high):
    def one(i, carry):
        low, high = carry
        wl, wh = w_low[i], w_high[i]
        for e in range(2):
            patch = moved[2 * i + e].astype(F32)
            low = low + patch * wl[e : e + 1]
            high = high + patch * wh[e : e + 1]
        return low, high

    return lax.fori_loop(0, PAIRS, one, (low, high), unroll=2)


def first_kernel(got, tiles, right, left, rows, msg, spec, moved, phase, info, table, along, w_low, w_high):
    flat = got[:, CAP * N :, :].astype(F32).reshape(C * 16, N)
    row, lane = iota((C * 16, N), 0), iota((C * 16, N), 1)
    info[...] = flat.reshape(PAIRS, 8, N)
    amount = jnp.where((row[:, 0:1] & 7) < 4, flat[:, 1:2], flat[:, 2:3]).astype(I32) & (N - 1)
    wave = dot((lane == amount).astype(BF16), rows[...])
    phase[...] = jnp.where((row & 3) < 2, wave[:, :N], wave[:, N:]).reshape(PAIRS, 8, N)

    def one(i, carry):
        at = pl.multiple_of((i % 2) * 2 * N, 2 * N)
        pair = got[i // 2, pl.ds(at, 2 * N), :]
        both = transform_pair(pair, right[...], left[...])
        spec[i] = both
        text = info[i]
        for e in range(2):
            down = (-text[e, 1].astype(I32)) & (N - 1)
            across = (-text[e, 2].astype(I32)) & (N - 1)
            patch = pltpu.roll(pair[e * N : (e + 1) * N].astype(F32), down, 0)
            moved[2 * i + e] = pltpu.roll(patch, across, 1).astype(BF16)
        return carry

    lax.fori_loop(0, PAIRS, one, 0, unroll=8)
    match(spec, tiles, info, phase, along)
    scores, low_sum, high_sum = weigh(along, info, w_low, w_high, 0)
    table[...] = scores
    zero = jnp.zeros((N, N), F32)
    low, high = weighted(moved, w_low, w_high, zero, zero)
    lines = [jnp.broadcast_to(v, (1, N)) for s in (low_sum, high_sum) for v in pieces(s)]
    tail = jnp.concatenate(lines + [jnp.zeros((10, N), F32)], 0).astype(BF16)
    low, high = low.astype(BF16), high.astype(BF16)
    for b in range(C):
        msg[b, :N, :] = low
        msg[b, N : 2 * N, :] = high
        msg[b, 2 * N :, :] = tail


def second_kernel(ids, got, old, spec, moved, phase, info, table, right, left, msg, tables_out, along, w_low, w_high, tiles):
    total = jnp.zeros((2 * N, N), F32)
    tail = jnp.zeros((16, N), F32)
    for b in range(C):
        total = total + got[b, : 2 * N, :].astype(F32)
        tail = tail + got[b, 2 * N :, :].astype(F32)
    fresh = []
    for p in range(PD):
        count = tail[3 * p : 3 * p + 1] + tail[3 * p + 1 : 3 * p + 2] + tail[3 * p + 2 : 3 * p + 3]
        part = old[p * N : (p + 1) * N, :].astype(F32) + total[p * N : (p + 1) * N]
        fresh.append((part / (1.0 + count)).astype(BF16))
    tiles[...] = transform_pair(jnp.concatenate(fresh, 0), right[...], left[...])
    match(spec, tiles, info, phase, along)
    scores, low_sum, high_sum = weigh(along, info, w_low, w_high, 1)
    tables_out[...] = table[...] + scores
    own = jnp.where(ids[0] == 0, 1.0, 0.0)
    low, high = weighted(
        moved, w_low, w_high, fresh[0].astype(F32) * own, fresh[1].astype(F32) * own
    )
    lines = [jnp.broadcast_to(s + own, (1, N)) for s in (low_sum, high_sum)]
    tail = jnp.concatenate(lines + [jnp.zeros((6, N), F32)], 0)
    msg[...] = jnp.zeros_like(msg)
    for b in range(C):
        at = ids[1] * C + b
        msg[at, :SLAB, :] = low[b * SLAB : (b + 1) * SLAB]
        msg[at, SLAB : 2 * SLAB, :] = high[b * SLAB : (b + 1) * SLAB]
        msg[at, 2 * SLAB :, :] = tail


def finish_kernel(ids, got, table, msg):
    total = got[ids[1] * C]
    for b in range(1, C):
        total = total + got[ids[1] * C + b]
    slab = jnp.concatenate(
        [
            total[p * SLAB : (p + 1) * SLAB] / total[2 * SLAB + p : 2 * SLAB + p + 1]
            for p in range(PD)
        ],
        0,
    ).astype(BF16)
    parts = pieces(table[...])
    pad = jnp.zeros((5, N), F32)
    for v in range(C):
        lines = jnp.concatenate([part[v : v + 1] for part in parts] + [pad], 0).astype(BF16)
        for y in range(C):
            msg[y * C + v, : 2 * SLAB, :] = slab
            msg[y * C + v, 2 * SLAB :, :] = lines


def place_kernel(ids, got, out, scores):
    for y in range(C):
        for g in range(C):
            for p in range(PD):
                out[PD * g + p, y * SLAB : (y + 1) * SLAB, :] = got[
                    y * C + g, p * SLAB : (p + 1) * SLAB, :
                ]
    total = jnp.zeros((8, N), F32)
    for c in range(C):
        total = total + got[ids[0] * C + c, 2 * SLAB :, :].astype(F32)
    scores[...] = total[0:1] + total[1:2] + total[2:3]


def call(kernel, outs, ins, scratch, args, flops=1e8):
    spaces = {"s": pltpu.SMEM, "v": pltpu.VMEM}
    size = sum(int(np.prod(o.shape)) * o.dtype.itemsize for o in outs)
    return pl.pallas_call(
        kernel,
        out_shape=outs,
        in_specs=[pl.BlockSpec(memory_space=spaces[i]) for i in ins],
        out_specs=[pl.BlockSpec(memory_space=pltpu.VMEM) for _ in outs],
        scratch_shapes=scratch,
        compiler_params=pltpu.CompilerParams(vmem_limit_bytes=40 << 20),
        cost_estimate=pl.CostEstimate(
            flops=int(flops), bytes_accessed=size + (1 << 20), transcendentals=0
        ),
    )(*args)


def struct(shape, dtype):
    return jax.ShapeDtypeStruct(shape, dtype)


def number(y, z, q):
    return (y * C + z) * C + q


def along_z():
    return [[y * C + z for z in range(C)] for y in range(C)]


def along_y():
    return [[y * C + z for y in range(C)] for z in range(C)]


def across():
    line = lambda z, q: [number(y, z, q) for y in range(C)]
    groups = [line(a, b) + line(b, a) for a in range(C) for b in range(a + 1, C)]
    return groups + [line(a, a) + line(a + 1, a + 1) for a in range(0, C, 2)]


def exchange(value, axis, groups=None):
    return lax.all_to_all(
        value, axis, split_axis=0, concat_axis=0, axis_index_groups=groups, tiled=True
    )


def local(frames, offsets, assign, residual, template):
    right, left, rows = (jnp.asarray(t) for t in tables())
    off = offsets.reshape(PD, 2)
    asg = assign.reshape(PD, C)
    res = residual.reshape(PD, C, 2).transpose(0, 2, 1)
    t = lax.axis_index("tm").astype(I32)
    q = lax.axis_index("plane").astype(I32)
    y, z = t >> 3, t & 7
    half = jnp.where(z == q, z & 1, (z < q).astype(I32))
    ids = jnp.stack([y, half])
    small = (PAIRS, 8, N)
    (dealt,) = call(
        deal_kernel,
        [struct((C, ROWS, N), BF16)],
        "sssv",
        [
            pltpu.VMEM((PD, N, C * N), BF16),
            pltpu.VMEM((C * CAP // 2, 8, N), F32),
            pltpu.SMEM((C,), I32),
        ],
        (off, asg, res, frames[0]),
    )
    got = exchange(dealt, "tm", along_z())
    swap = [
        (number(a, b, c), number(a, c, b)) for a in range(C) for b in range(C) for c in range(C)
    ]
    mine = lax.dynamic_slice_in_dim(template, PD * z, PD, 0).reshape(PD * N, N)
    old = lax.ppermute(mine, ("tm", "plane"), swap)
    (tiles,) = call(tile_kernel, [struct((2 * N, 2 * N), F32)], "vvv", [], (old, right, left))
    scratch = [pltpu.VMEM(small, F32) for _ in range(3)]
    msg, spec, moved, phase, info, table = call(
        first_kernel,
        [
            struct((C, 2 * N + 16, N), BF16),
            struct((PAIRS, 2 * N, 2 * N), F32),
            struct((2 * PAIRS, N, N), BF16),
            struct(small, F32),
            struct(small, F32),
            struct((C, N), F32),
        ],
        "vvvvv",
        scratch,
        (got, tiles, right, left, rows),
        flops=1e9,
    )
    got = exchange(msg, "tm", along_y())
    msg, table = call(
        second_kernel,
        [struct((2 * C, 2 * SLAB + 8, N), F32), struct((C, N), F32)],
        "svvvvvvvvv",
        scratch + [pltpu.VMEM((2 * N, 2 * N), F32)],
        (ids, got, old, spec, moved, phase, info, table, right, left),
        flops=1e9,
    )
    got = exchange(msg, ("tm", "plane"), across())
    (msg,) = call(
        finish_kernel, [struct((C * C, 2 * SLAB + 8, N), BF16)], "svv", [], (ids, got, table)
    )
    got = exchange(msg, "tm")
    out, scores = call(
        place_kernel, [struct((PD * C, N, N), BF16), struct((1, N), F32)], "sv", [], (ids, got)
    )
    return out, scores[0, : 2 * PD * C].reshape(2, 1, PD, 1, C)


def solution(mesh):
    return jax.shard_map(
        local,
        mesh=mesh,
        in_specs=(
            P("tm", "plane", None, None),
            P("tm", "plane", None),
            P("tm", "plane", None, None, None),
            P("tm", "plane", None, None, None),
            P(None, None, "plane"),
        ),
        out_specs=(P(None, None, "plane"), P(None, "tm", "plane", None, None)),
        check_vma=False,
    )
```

```python
import jax
import jax.numpy as jnp
import numpy as np
from jax import lax
from jax.experimental import pallas as pl
from jax.experimental.pallas import tpu as pltpu
from jax.sharding import PartitionSpec as P


N = 128
C = 8
PD = 2
CAP = 4
PAIRS = C * CAP // 2
ROWS = CAP * N + 16
SLAB = N // C
F32, BF16, I32 = jnp.float32, jnp.bfloat16, jnp.int32


def tables():
    j = np.arange(N, dtype=np.int32)
    phase = (j[:, None] * j[None, :] % N).astype(np.float32) * np.float32(2.0 * np.pi / N)
    cos = np.cos(phase).astype(BF16)
    sin = np.sin(phase).astype(BF16)
    right = np.concatenate([cos, -sin], 1)
    left = np.concatenate(
        [np.concatenate([cos, sin], 1), np.concatenate([-sin, cos], 1)], 0
    )
    rows = np.concatenate([cos, sin], 1)
    return right, left, rows


def dot(a, b):
    return jnp.dot(a, b, preferred_element_type=F32)


def transform_pair(pair, right, left):
    first = dot(pair, right).astype(BF16)
    inner = jnp.concatenate(
        [
            jnp.concatenate([first[:N, :N], first[N:, :N]], 1),
            jnp.concatenate([first[:N, N:], first[N:, N:]], 1),
        ],
        0,
    )
    return dot(left, inner)


def pieces(value):
    high = value.astype(BF16).astype(F32)
    rest = value - high
    mid = rest.astype(BF16).astype(F32)
    return high, mid, rest - mid


def iota(shape, axis):
    return lax.broadcasted_iota(I32, shape, axis)


def deal_kernel(ids, off_in, asg_in, res_in, frames_in, out, frames, off, asg, res, shifted, details, count, sems):
    copies = [
        pltpu.make_async_copy(source, target, sems.at[i])
        for i, (source, target) in enumerate(
            ((off_in, off), (asg_in, asg), (res_in, res), (frames_in, frames))
        )
    ]
    for copy in copies:
        copy.start()
    out[...] = jnp.zeros_like(out)
    details[...] = jnp.zeros_like(details)
    for c in range(C):
        count[c] = 0
    for copy in copies:
        copy.wait()
    for p in range(PD):
        plane = frames[p].astype(F32)
        plane = pltpu.roll(plane, (-off[p, 0]) & (N - 1), 0)
        plane = pltpu.roll(plane, (-off[p, 1]) & (C * N - 1), 1)
        shifted[p] = plane.astype(BF16)
    lane, row = iota((8, N), 1), iota((8, N), 0)
    for p in range(PD):
        for k in range(C):
            c = (asg[p, k] + ids[2]) & (C - 1)
            slot = count[c]
            count[c] = slot + 1
            at = pl.multiple_of(slot * N, N)
            out[c, pl.ds(at, N), :] = shifted[p, :, k * N : (k + 1) * N]
            text = jnp.where(lane == 0, p, 0)
            text = jnp.where(lane == 1, res[p, 0, k], text)
            text = jnp.where(lane == 2, res[p, 1, k], text)
            text = jnp.where(lane == 3, 1, text)
            text = jnp.where(lane == 4, p * C + k, text).astype(F32)
            at = c * (CAP // 2) + slot // 2
            details[at] = jnp.where((row & 1) == (slot & 1), text, details[at])
    for c in range(C):
        for j in range(CAP // 2):
            out[c, CAP * N + 8 * j : CAP * N + 8 * (j + 1), :] = details[
                c * (CAP // 2) + j
            ].astype(BF16)


def tile_kernel(pair, right, left, spec):
    spec[...] = transform_pair(pair[...], right[...], left[...])


def along_of(both, tiles, info, phase):
    outs = []
    for e in range(2):
        p_re, p_im = both[:N, e * N : (e + 1) * N], both[N:, e * N : (e + 1) * N]
        upper = info[e : e + 1, 0:1] > 0.5
        t_re = jnp.where(upper, tiles[:N, N:], tiles[:N, :N])
        t_im = jnp.where(upper, tiles[N:, N:], tiles[N:, :N])
        c_re = p_re * t_re + p_im * t_im
        c_im = p_im * t_re - p_re * t_im
        modulus = jnp.sqrt(c_re * c_re + c_im * c_im)
        level = jnp.sum(jnp.sum(modulus, 0, keepdims=True), 1, keepdims=True) * (1.0 / (N * N))
        scale = 1.0 / (modulus + 0.1 * level + 1e-06)
        n_re = (c_re * scale).astype(BF16)
        n_im = (c_im * scale).astype(BF16)
        lhs = jnp.concatenate([phase[e : e + 1], phase[2 + e : 3 + e]], 0).astype(BF16)
        s_re, s_im = dot(lhs, n_re), dot(lhs, n_im)
        outs.append(
            phase[4 + e : 5 + e] * (s_re[0:1] - s_im[1:2])
            - phase[6 + e : 7 + e] * (s_re[1:2] + s_im[0:1])
        )
    return jnp.concatenate(outs, 0)


def match(spec, tiles, info, phase, along):
    along[...] = jnp.zeros_like(along)

    def one(i, carry):
        along[i, 0:2, :] = along_of(spec[i], tiles[...], info[i], phase[i])
        return carry

    lax.fori_loop(0, PAIRS, one, 0, unroll=8)


def weigh(along, info, w_low, w_high, turn):
    flat = info[...].reshape(C * 16, N)
    row = iota((C * 16, 1), 0)
    live = jnp.where((row & 7) < 2, flat[:, 3:4], 0.0)
    score = jnp.sum(along[...].reshape(C * 16, N), 1, keepdims=True) * (1.0 / N)
    weight = (0.5 + 1.0 / (1.0 + jnp.exp(-score))) * live
    high = weight * flat[:, 0:1]
    low = weight - high
    w_low[...] = jnp.broadcast_to(low, (C * 16, N)).reshape(PAIRS, 8, N)
    w_high[...] = jnp.broadcast_to(high, (C * 16, N)).reshape(PAIRS, 8, N)
    lane = iota((C * 16, N), 1)
    at = flat[:, 4:5].astype(I32) + turn * 16
    table = jnp.where(lane == at, score * live, 0.0).reshape(C, 16, N)
    return jnp.sum(table, 1), jnp.sum(low, 0, keepdims=True), jnp.sum(high, 0, keepdims=True)


def weighted(moved, w_low, w_high, low, high):
    def one(i, carry):
        low, high = carry
        wl, wh = w_low[i], w_high[i]
        for e in range(2):
            patch = moved[2 * i + e].astype(F32)
            low = low + patch * wl[e : e + 1]
            high = high + patch * wh[e : e + 1]
        return low, high

    return lax.fori_loop(0, PAIRS, one, (low, high), unroll=2)


def first_kernel(got, tiles, right, left, rows, msg, spec, moved, phase, info, table, along, w_low, w_high):
    flat = got[:, CAP * N :, :].astype(F32).reshape(C * 16, N)
    row, lane = iota((C * 16, N), 0), iota((C * 16, N), 1)
    info[...] = flat.reshape(PAIRS, 8, N)
    amount = jnp.where((row[:, 0:1] & 7) < 4, flat[:, 1:2], flat[:, 2:3]).astype(I32) & (N - 1)
    wave = dot((lane == amount).astype(BF16), rows[...])
    phase[...] = jnp.where((row & 3) < 2, wave[:, :N], wave[:, N:]).reshape(PAIRS, 8, N)

    def one(i, carry):
        at = pl.multiple_of((i % 2) * 2 * N, 2 * N)
        pair = got[i // 2, pl.ds(at, 2 * N), :]
        both = transform_pair(pair, right[...], left[...])
        spec[i] = both
        text = info[i]
        for e in range(2):
            down = (-text[e, 1].astype(I32)) & (N - 1)
            across = (-text[e, 2].astype(I32)) & (N - 1)
            patch = pltpu.roll(pair[e * N : (e + 1) * N].astype(F32), down, 0)
            moved[2 * i + e] = pltpu.roll(patch, across, 1).astype(BF16)
        return carry

    lax.fori_loop(0, PAIRS, one, 0, unroll=8)
    match(spec, tiles, info, phase, along)
    scores, low_sum, high_sum = weigh(along, info, w_low, w_high, 0)
    table[...] = scores
    zero = jnp.zeros((N, N), F32)
    low, high = weighted(moved, w_low, w_high, zero, zero)
    lines = [jnp.broadcast_to(v, (1, N)) for s in (low_sum, high_sum) for v in pieces(s)]
    tail = jnp.concatenate(lines + [jnp.zeros((10, N), F32)], 0).astype(BF16)
    low, high = low.astype(BF16), high.astype(BF16)
    for b in range(C):
        msg[b, :N, :] = low
        msg[b, N : 2 * N, :] = high
        msg[b, 2 * N :, :] = tail


def second_kernel(ids, got, old, spec, moved, phase, info, table, right, left, msg, tables_out, along, w_low, w_high, tiles):
    total = jnp.zeros((2 * N, N), F32)
    tail = jnp.zeros((16, N), F32)
    for b in range(C):
        total = total + got[b, : 2 * N, :].astype(F32)
        tail = tail + got[b, 2 * N :, :].astype(F32)
    fresh = []
    for p in range(PD):
        count = tail[3 * p : 3 * p + 1] + tail[3 * p + 1 : 3 * p + 2] + tail[3 * p + 2 : 3 * p + 3]
        part = old[p * N : (p + 1) * N, :].astype(F32) + total[p * N : (p + 1) * N]
        fresh.append((part / (1.0 + count)).astype(BF16))
    tiles[...] = transform_pair(jnp.concatenate(fresh, 0), right[...], left[...])
    match(spec, tiles, info, phase, along)
    scores, low_sum, high_sum = weigh(along, info, w_low, w_high, 1)
    tables_out[...] = table[...] + scores
    own = jnp.where(ids[0] == 0, 1.0, 0.0)
    low, high = weighted(
        moved, w_low, w_high, fresh[0].astype(F32) * own, fresh[1].astype(F32) * own
    )
    lines = [jnp.broadcast_to(s + own, (1, N)) for s in (low_sum, high_sum)]
    tail = jnp.concatenate(lines + [jnp.zeros((6, N), F32)], 0)
    msg[...] = jnp.zeros_like(msg)
    for b in range(C):
        at = ids[1] * C + b
        msg[at, :SLAB, :] = low[b * SLAB : (b + 1) * SLAB]
        msg[at, SLAB : 2 * SLAB, :] = high[b * SLAB : (b + 1) * SLAB]
        msg[at, 2 * SLAB :, :] = tail


def finish_kernel(ids, got, table, msg):
    total = got[ids[1] * C]
    for b in range(1, C):
        total = total + got[ids[1] * C + b]
    slab = jnp.concatenate(
        [
            total[p * SLAB : (p + 1) * SLAB] / total[2 * SLAB + p : 2 * SLAB + p + 1]
            for p in range(PD)
        ],
        0,
    ).astype(BF16)
    parts = pieces(table[...])
    pad = jnp.zeros((5, N), F32)
    for v in range(C):
        lines = jnp.concatenate([part[v : v + 1] for part in parts] + [pad], 0).astype(BF16)
        for y in range(C):
            msg[y * C + v, : 2 * SLAB, :] = slab
            msg[y * C + v, 2 * SLAB :, :] = lines


def place_kernel(ids, got, out, scores):
    for y in range(C):
        for z in range(C):
            group = (z - ids[2]) & (C - 1)
            for p in range(PD):
                out[PD * group + p, y * SLAB : (y + 1) * SLAB, :] = got[
                    y * C + z, p * SLAB : (p + 1) * SLAB, :
                ]
    total = jnp.zeros((8, N), F32)
    for c in range(C):
        total = total + got[ids[0] * C + c, 2 * SLAB :, :].astype(F32)
    line = total[0:1] + total[1:2] + total[2:3]
    for j in range(2 * PD):
        scores[j // PD, 0, j % PD, :, :] = line[:, j * C : (j + 1) * C]


def call(kernel, outs, ins, scratch, args, flops=1e8, grant=16):
    spaces = {"s": pltpu.SMEM, "v": pltpu.VMEM, "h": pltpu.HBM}
    size = sum(int(np.prod(o.shape)) * o.dtype.itemsize for o in outs)
    return pl.pallas_call(
        kernel,
        out_shape=outs,
        in_specs=[pl.BlockSpec(memory_space=spaces[i]) for i in ins],
        out_specs=[pl.BlockSpec(memory_space=pltpu.VMEM) for _ in outs],
        scratch_shapes=scratch,
        compiler_params=pltpu.CompilerParams(vmem_limit_bytes=grant << 20),
        cost_estimate=pl.CostEstimate(
            flops=int(flops), bytes_accessed=size + (1 << 20), transcendentals=0
        ),
    )(*args)


def struct(shape, dtype):
    return jax.ShapeDtypeStruct(shape, dtype)


def number(y, z, q):
    return (y * C + z) * C + q


def along_z():
    return [[y * C + z for z in range(C)] for y in range(C)]


def along_y():
    return [[y * C + z for y in range(C)] for z in range(C)]


def across():
    groups = []
    for z in range(C):
        pairs = [(a, (z - a) % C) for a in range(C) if a < (z - a) % C]
        if z % 2 == 0:
            pairs.append((z // 2, z // 2 + C // 2))
        for pair in pairs:
            groups.append([number(y, z, q) for q in pair for y in range(C)])
    return groups


def exchange(value, axis, groups=None):
    return lax.all_to_all(
        value, axis, split_axis=0, concat_axis=0, axis_index_groups=groups, tiled=True
    )


def local(frames, offsets, assign, residual, template):
    right, left, rows = (jnp.asarray(t) for t in tables())
    off = offsets.reshape(PD, 2)
    asg = assign.reshape(PD, C)
    res = residual.reshape(PD, C, 2).transpose(0, 2, 1)
    t = lax.axis_index("tm").astype(I32)
    q = lax.axis_index("plane").astype(I32)
    y, z = t >> 3, t & 7
    other = (z - q) & (C - 1)
    half = jnp.where(other == q, q >> 2, (q < other).astype(I32))
    ids = jnp.stack([y, half, q])
    small = (PAIRS, 8, N)
    (dealt,) = call(
        deal_kernel,
        [struct((C, ROWS, N), BF16)],
        "shhhh",
        [
            pltpu.VMEM((PD, N, C * N), BF16),
            pltpu.SMEM((PD, 2), I32),
            pltpu.SMEM((PD, C), I32),
            pltpu.SMEM((PD, 2, C), I32),
            pltpu.VMEM((PD, N, C * N), BF16),
            pltpu.VMEM((C * CAP // 2, 8, N), F32),
            pltpu.SMEM((C,), I32),
            pltpu.SemaphoreType.DMA((4,)),
        ],
        (ids, off, asg, res, frames[0]),
        grant=63,
    )
    got = exchange(dealt, "tm", along_z())
    swap = [
        (number(a, b, c), number(a, b, (b - c) % C))
        for a in range(C)
        for b in range(C)
        for c in range(C)
    ]
    mine = lax.dynamic_slice_in_dim(template, PD * other, PD, 0).reshape(PD * N, N)
    old = lax.ppermute(mine, ("tm", "plane"), swap)
    (tiles,) = call(tile_kernel, [struct((2 * N, 2 * N), F32)], "vvv", [], (old, right, left))
    scratch = [pltpu.VMEM(small, F32) for _ in range(3)]
    msg, spec, moved, phase, info, table = call(
        first_kernel,
        [
            struct((C, 2 * N + 16, N), BF16),
            struct((PAIRS, 2 * N, 2 * N), F32),
            struct((2 * PAIRS, N, N), BF16),
            struct(small, F32),
            struct(small, F32),
            struct((C, N), F32),
        ],
        "vvvvv",
        scratch,
        (got, tiles, right, left, rows),
        flops=1e9,
    )
    got = exchange(msg, "tm", along_y())
    msg, table = call(
        second_kernel,
        [struct((2 * C, 2 * SLAB + 8, N), F32), struct((C, N), F32)],
        "svvvvvvvvv",
        scratch + [pltpu.VMEM((2 * N, 2 * N), F32)],
        (ids, got, old, spec, moved, phase, info, table, right, left),
        flops=1e9,
    )
    got = exchange(msg, ("tm", "plane"), across())
    (msg,) = call(
        finish_kernel, [struct((C * C, 2 * SLAB + 8, N), BF16)], "svv", [], (ids, got, table)
    )
    got = exchange(msg, "tm")
    out, scores = call(
        place_kernel,
        [struct((PD * C, N, N), BF16), struct((2, 1, PD, 1, C), F32)],
        "sv",
        [],
        (ids, got),
    )
    return out, scores


def solution(mesh):
    return jax.shard_map(
        local,
        mesh=mesh,
        in_specs=(
            P("tm", "plane", None, None),
            P("tm", "plane", None),
            P("tm", "plane", None, None, None),
            P("tm", "plane", None, None, None),
            P(None, None, "plane"),
        ),
        out_specs=(P(None, None, "plane"), P(None, "tm", "plane", None, None)),
        check_vma=False,
    )
```

```python
import jax
import jax.numpy as jnp
import numpy as np
from jax import lax
from jax.experimental import pallas as pl
from jax.experimental.pallas import tpu as pltpu
from jax.sharding import PartitionSpec as P


N = 128
C = 8
PD = 2
CAP = 4
PAIRS = C * CAP // 2
ROWS = CAP * N + 16
SLAB = N // C
F32, BF16, I32 = jnp.float32, jnp.bfloat16, jnp.int32


def tables():
    j = np.arange(N, dtype=np.int32)
    phase = (j[:, None] * j[None, :] % N).astype(np.float32) * np.float32(2.0 * np.pi / N)
    cos = np.cos(phase).astype(BF16)
    sin = np.sin(phase).astype(BF16)
    right = np.concatenate([cos, -sin], 1)
    left = np.concatenate(
        [np.concatenate([cos, sin], 1), np.concatenate([-sin, cos], 1)], 0
    )
    rows = np.concatenate([cos, sin], 1)
    return right, left, rows


def dot(a, b):
    return jnp.dot(a, b, preferred_element_type=F32)


def transform_pair(pair, right, left):
    first = dot(pair, right).astype(BF16)
    inner = jnp.concatenate(
        [
            jnp.concatenate([first[:N, :N], first[N:, :N]], 1),
            jnp.concatenate([first[:N, N:], first[N:, N:]], 1),
        ],
        0,
    )
    return dot(left, inner)


def pieces(value):
    high = value.astype(BF16).astype(F32)
    rest = value - high
    mid = rest.astype(BF16).astype(F32)
    return high, mid, rest - mid


def place():
    t = lax.axis_index("tm").astype(I32)
    return t >> 3, t & (C - 1), lax.axis_index("plane").astype(I32)


def own_half():
    _, z, q = place()
    other = (z - q) & (C - 1)
    return jnp.where(other == q, q >> 2, jnp.where(q < other, 1, 0)) * C


def iota(shape, axis):
    return lax.broadcasted_iota(I32, shape, axis)


def deal_kernel(off_in, asg_in, res_in, frames_in, out, frames, off, asg, res, shifted, details, count, sems):
    copies = [
        pltpu.make_async_copy(source, target, sems.at[i])
        for i, (source, target) in enumerate(
            ((off_in, off), (asg_in, asg), (res_in, res), (frames_in, frames))
        )
    ]
    for copy in copies:
        copy.start()
    out[...] = jnp.zeros_like(out)
    details[...] = jnp.zeros_like(details)
    for c in range(C):
        count[c] = 0
    for copy in copies:
        copy.wait()
    for p in range(PD):
        plane = frames[p].astype(F32)
        plane = pltpu.roll(plane, (-off[p, 0]) & (N - 1), 0)
        plane = pltpu.roll(plane, (-off[p, 1]) & (C * N - 1), 1)
        shifted[p] = plane.astype(BF16)
    lane, row = iota((8, N), 1), iota((8, N), 0)
    for p in range(PD):
        for k in range(C):
            c = (asg[p, k] + place()[2]) & (C - 1)
            slot = count[c]
            count[c] = slot + 1
            at = pl.multiple_of(slot * N, N)
            out[c, pl.ds(at, N), :] = shifted[p, :, k * N : (k + 1) * N]
            text = jnp.where(lane == 0, p, 0)
            text = jnp.where(lane == 1, res[p, 0, k], text)
            text = jnp.where(lane == 2, res[p, 1, k], text)
            text = jnp.where(lane == 3, 1, text)
            text = jnp.where(lane == 4, p * C + k, text).astype(F32)
            at = c * (CAP // 2) + slot // 2
            details[at] = jnp.where((row & 1) == (slot & 1), text, details[at])
    for c in range(C):
        for j in range(CAP // 2):
            out[c, CAP * N + 8 * j : CAP * N + 8 * (j + 1), :] = details[
                c * (CAP // 2) + j
            ].astype(BF16)


def tile_kernel(pair, right, left, spec):
    spec[...] = transform_pair(pair[...], right[...], left[...])


def along_of(both, tiles, info, phase):
    outs = []
    for e in range(2):
        p_re, p_im = both[:N, e * N : (e + 1) * N], both[N:, e * N : (e + 1) * N]
        upper = info[e : e + 1, 0:1] > 0.5
        t_re = jnp.where(upper, tiles[:N, N:], tiles[:N, :N])
        t_im = jnp.where(upper, tiles[N:, N:], tiles[N:, :N])
        c_re = p_re * t_re + p_im * t_im
        c_im = p_im * t_re - p_re * t_im
        modulus = jnp.sqrt(c_re * c_re + c_im * c_im)
        level = jnp.sum(jnp.sum(modulus, 0, keepdims=True), 1, keepdims=True) * (1.0 / (N * N))
        scale = 1.0 / (modulus + 0.1 * level + 1e-06)
        n_re = (c_re * scale).astype(BF16)
        n_im = (c_im * scale).astype(BF16)
        lhs = jnp.concatenate([phase[e : e + 1], phase[2 + e : 3 + e]], 0).astype(BF16)
        s_re, s_im = dot(lhs, n_re), dot(lhs, n_im)
        outs.append(
            phase[4 + e : 5 + e] * (s_re[0:1] - s_im[1:2])
            - phase[6 + e : 7 + e] * (s_re[1:2] + s_im[0:1])
        )
    return jnp.concatenate(outs, 0)


def match(spec, tiles, info, phase, along):
    along[...] = jnp.zeros_like(along)

    def one(i, carry):
        along[i, 0:2, :] = along_of(spec[i], tiles[...], info[i], phase[i])
        return carry

    lax.fori_loop(0, PAIRS, one, 0, unroll=8)


def weigh(along, info, w_low, w_high, turn):
    flat = info[...].reshape(C * 16, N)
    row = iota((C * 16, 1), 0)
    live = jnp.where((row & 7) < 2, flat[:, 3:4], 0.0)
    score = jnp.sum(along[...].reshape(C * 16, N), 1, keepdims=True) * (1.0 / N)
    weight = (0.5 + 1.0 / (1.0 + jnp.exp(-score))) * live
    high = weight * flat[:, 0:1]
    low = weight - high
    w_low[...] = jnp.broadcast_to(low, (C * 16, N)).reshape(PAIRS, 8, N)
    w_high[...] = jnp.broadcast_to(high, (C * 16, N)).reshape(PAIRS, 8, N)
    lane = iota((C * 16, N), 1)
    at = flat[:, 4:5].astype(I32) + turn * 16
    table = jnp.where(lane == at, score * live, 0.0).reshape(C, 16, N)
    return jnp.sum(table, 1), jnp.sum(low, 0, keepdims=True), jnp.sum(high, 0, keepdims=True)


def weighted(moved, w_low, w_high, low, high):
    def one(i, carry):
        low, high = carry
        wl, wh = w_low[i], w_high[i]
        for e in range(2):
            patch = moved[2 * i + e].astype(F32)
            low = low + patch * wl[e : e + 1]
            high = high + patch * wh[e : e + 1]
        return low, high

    return lax.fori_loop(0, PAIRS, one, (low, high), unroll=2)


def first_kernel(got, tiles, right, left, rows, msg, spec, moved, phase, info, table, along, w_low, w_high):
    flat = got[:, CAP * N :, :].astype(F32).reshape(C * 16, N)
    row, lane = iota((C * 16, N), 0), iota((C * 16, N), 1)
    info[...] = flat.reshape(PAIRS, 8, N)
    amount = jnp.where((row[:, 0:1] & 7) < 4, flat[:, 1:2], flat[:, 2:3]).astype(I32) & (N - 1)
    wave = dot((lane == amount).astype(BF16), rows[...])
    phase[...] = jnp.where((row & 3) < 2, wave[:, :N], wave[:, N:]).reshape(PAIRS, 8, N)

    def one(i, carry):
        at = pl.multiple_of((i % 2) * 2 * N, 2 * N)
        pair = got[i // 2, pl.ds(at, 2 * N), :]
        both = transform_pair(pair, right[...], left[...])
        spec[i] = both
        text = info[i]
        for e in range(2):
            down = (-text[e, 1].astype(I32)) & (N - 1)
            across = (-text[e, 2].astype(I32)) & (N - 1)
            patch = pltpu.roll(pair[e * N : (e + 1) * N].astype(F32), down, 0)
            moved[2 * i + e] = pltpu.roll(patch, across, 1).astype(BF16)
        return carry

    lax.fori_loop(0, PAIRS, one, 0, unroll=8)
    match(spec, tiles, info, phase, along)
    scores, low_sum, high_sum = weigh(along, info, w_low, w_high, 0)
    table[...] = scores
    zero = jnp.zeros((N, N), F32)
    low, high = weighted(moved, w_low, w_high, zero, zero)
    lines = [jnp.broadcast_to(v, (1, N)) for s in (low_sum, high_sum) for v in pieces(s)]
    tail = jnp.concatenate(lines + [jnp.zeros((2, N), F32)], 0).astype(BF16)
    low, high = low.astype(BF16), high.astype(BF16)
    for b in range(C):
        msg[b, :N, :] = low
        msg[b, N : 2 * N, :] = high
        msg[b, 2 * N :, :] = tail


def second_kernel(got, old, spec, moved, phase, info, table, right, left, msg, tables_out, along, w_low, w_high, tiles):
    total = jnp.zeros((2 * N, N), F32)
    tail = jnp.zeros((8, N), F32)
    for b in range(C):
        total = total + got[b, : 2 * N, :].astype(F32)
        tail = tail + got[b, 2 * N :, :].astype(F32)
    fresh = []
    for p in range(PD):
        count = tail[3 * p : 3 * p + 1] + tail[3 * p + 1 : 3 * p + 2] + tail[3 * p + 2 : 3 * p + 3]
        part = old[p * N : (p + 1) * N, :].astype(F32) + total[p * N : (p + 1) * N]
        fresh.append((part / (1.0 + count)).astype(BF16))
    tiles[...] = transform_pair(jnp.concatenate(fresh, 0), right[...], left[...])
    match(spec, tiles, info, phase, along)
    scores, low_sum, high_sum = weigh(along, info, w_low, w_high, 1)
    tables_out[...] = table[...] + scores
    own = jnp.where(place()[0] == 0, 1.0, 0.0)
    low, high = weighted(
        moved, w_low, w_high, fresh[0].astype(F32) * own, fresh[1].astype(F32) * own
    )
    lines = [
        jnp.broadcast_to(v, (1, N)) for s in (low_sum, high_sum) for v in pieces(s + own)
    ]
    tail = jnp.concatenate(lines + [jnp.zeros((2, N), F32)], 0).astype(BF16)
    low, high = low.astype(BF16), high.astype(BF16)
    msg[...] = jnp.zeros_like(msg)
    half = own_half()
    for b in range(C):
        msg[half + b, :SLAB, :] = low[b * SLAB : (b + 1) * SLAB]
        msg[half + b, SLAB : 2 * SLAB, :] = high[b * SLAB : (b + 1) * SLAB]
        msg[half + b, 2 * SLAB :, :] = tail


def finish_kernel(got, table, msg):
    half = own_half()
    total = got[half].astype(F32)
    for b in range(1, C):
        total = total + got[half + b].astype(F32)
    tail = total[2 * SLAB :]
    slab = []
    for p in range(PD):
        count = tail[3 * p : 3 * p + 1] + tail[3 * p + 1 : 3 * p + 2] + tail[3 * p + 2 : 3 * p + 3]
        slab.append(total[p * SLAB : (p + 1) * SLAB] / count)
    slab = jnp.concatenate(slab, 0).astype(BF16)
    parts = pieces(table[...])
    pad = jnp.zeros((5, N), F32)
    for v in range(C):
        lines = jnp.concatenate([part[v : v + 1] for part in parts] + [pad], 0).astype(BF16)
        for y in range(C):
            msg[y * C + v, : 2 * SLAB, :] = slab
            msg[y * C + v, 2 * SLAB :, :] = lines


def place_kernel(got, out, scores, sems):
    y, _, q = place()
    copies = []
    for z in range(C):
        group = (z - q) & (C - 1)
        for p in range(PD):
            copies.append(
                pltpu.make_async_copy(
                    got.at[:, z, p * SLAB : (p + 1) * SLAB, :],
                    out.at[PD * group + p],
                    sems.at[PD * z + p],
                )
            )
    for copy in copies:
        copy.start()
    total = jnp.zeros((8, N), F32)
    for c in range(C):
        total = total + got[y, c, 2 * SLAB :, :].astype(F32)
    line = total[0:1] + total[1:2] + total[2:3]
    for j in range(2 * PD):
        scores[j // PD, 0, j % PD, :, :] = line[:, j * C : (j + 1) * C]
    for copy in copies:
        copy.wait()


def call(kernel, outs, ins, scratch, args, flops=1e8, grant=16, spread=None):
    spaces = {"s": pltpu.SMEM, "v": pltpu.VMEM, "h": pltpu.HBM}
    size = sum(int(np.prod(o.shape)) * o.dtype.itemsize for o in outs)
    return pl.pallas_call(
        kernel,
        out_shape=outs,
        in_specs=[pl.BlockSpec(memory_space=spaces[i]) for i in ins],
        out_specs=[pl.BlockSpec(memory_space=spaces[o]) for o in spread or "v" * len(outs)],
        scratch_shapes=scratch,
        compiler_params=pltpu.CompilerParams(vmem_limit_bytes=grant << 20),
        cost_estimate=pl.CostEstimate(
            flops=int(flops), bytes_accessed=size + (1 << 20), transcendentals=0
        ),
    )(*args)


def struct(shape, dtype):
    return jax.ShapeDtypeStruct(shape, dtype)


def number(y, z, q):
    return (y * C + z) * C + q


def along_z():
    return [[y * C + z for z in range(C)] for y in range(C)]


def along_y():
    return [[y * C + z for y in range(C)] for z in range(C)]


def across():
    groups = []
    for z in range(C):
        pairs = [(a, (z - a) % C) for a in range(C) if a < (z - a) % C]
        if z % 2 == 0:
            pairs.append((z // 2, z // 2 + C // 2))
        for pair in pairs:
            groups.append([number(y, z, q) for q in pair for y in range(C)])
    return groups


def exchange(value, axis, groups=None):
    return lax.all_to_all(
        value, axis, split_axis=0, concat_axis=0, axis_index_groups=groups, tiled=True
    )


def local(frames, offsets, assign, residual, template):
    right, left, rows = (jnp.asarray(t) for t in tables())
    off = offsets.reshape(PD, 2)
    asg = assign.reshape(PD, C)
    res = residual.reshape(PD, C, 2).transpose(0, 2, 1)
    _, z, q = place()
    other = (z - q) & (C - 1)
    small = (PAIRS, 8, N)
    (dealt,) = call(
        deal_kernel,
        [struct((C, ROWS, N), BF16)],
        "hhhh",
        [
            pltpu.VMEM((PD, N, C * N), BF16),
            pltpu.SMEM((PD, 2), I32),
            pltpu.SMEM((PD, C), I32),
            pltpu.SMEM((PD, 2, C), I32),
            pltpu.VMEM((PD, N, C * N), BF16),
            pltpu.VMEM((C * CAP // 2, 8, N), F32),
            pltpu.SMEM((C,), I32),
            pltpu.SemaphoreType.DMA((4,)),
        ],
        (off, asg, res, frames[0]),
        grant=63,
    )
    got = exchange(dealt, "tm", along_z())
    swap = [
        (number(a, b, c), number(a, b, (b - c) % C))
        for a in range(C)
        for b in range(C)
        for c in range(C)
    ]
    mine = lax.dynamic_slice_in_dim(template, PD * other, PD, 0).reshape(PD * N, N)
    old = lax.ppermute(mine, ("tm", "plane"), swap)
    (tiles,) = call(tile_kernel, [struct((2 * N, 2 * N), F32)], "vvv", [], (old, right, left))
    scratch = [pltpu.VMEM(small, F32) for _ in range(3)]
    msg, spec, moved, phase, info, table = call(
        first_kernel,
        [
            struct((C, 2 * N + 8, N), BF16),
            struct((PAIRS, 2 * N, 2 * N), F32),
            struct((2 * PAIRS, N, N), BF16),
            struct(small, F32),
            struct(small, F32),
            struct((C, N), F32),
        ],
        "vvvvv",
        scratch,
        (got, tiles, right, left, rows),
        flops=1e9,
    )
    got = exchange(msg, "tm", along_y())
    msg, table = call(
        second_kernel,
        [struct((2 * C, 2 * SLAB + 8, N), BF16), struct((C, N), F32)],
        "vvvvvvvvv",
        scratch + [pltpu.VMEM((2 * N, 2 * N), F32)],
        (got, old, spec, moved, phase, info, table, right, left),
        flops=1e9,
    )
    got = exchange(msg, ("tm", "plane"), across())
    (msg,) = call(finish_kernel, [struct((C * C, 2 * SLAB + 8, N), BF16)], "vv", [], (got, table))
    got = exchange(msg, "tm")
    out, scores = call(
        place_kernel,
        [struct((PD * C, C, SLAB, N), BF16), struct((2, 1, PD, 1, C), F32)],
        "v",
        [pltpu.SemaphoreType.DMA((PD * C,))],
        (got.reshape(C, C, 2 * SLAB + 8, N),),
        spread="hv",
    )
    return out.reshape(PD * C, N, N), scores


def solution(mesh):
    return jax.shard_map(
        local,
        mesh=mesh,
        in_specs=(
            P("tm", "plane", None, None),
            P("tm", "plane", None),
            P("tm", "plane", None, None, None),
            P("tm", "plane", None, None, None),
            P(None, None, "plane"),
        ),
        out_specs=(P(None, None, "plane"), P(None, "tm", "plane", None, None)),
        check_vma=False,
    )
```

```python
import jax
import jax.numpy as jnp
import numpy as np
from jax import lax
from jax.experimental import pallas as pl
from jax.experimental.pallas import tpu as pltpu
from jax.sharding import PartitionSpec as P


N = 128
C = 8
PD = 2
CAP = 4
PAIRS = C * CAP // 2
ROWS = CAP * N + 16
SLAB = N // C
F32, BF16, I32 = jnp.float32, jnp.bfloat16, jnp.int32


def tables():
    j = np.arange(N, dtype=np.int32)
    phase = (j[:, None] * j[None, :] % N).astype(np.float32) * np.float32(2.0 * np.pi / N)
    cos = np.cos(phase).astype(BF16)
    sin = np.sin(phase).astype(BF16)
    right = np.concatenate([cos, -sin], 1)
    left = np.concatenate(
        [np.concatenate([cos, sin], 1), np.concatenate([-sin, cos], 1)], 0
    )
    rows = np.concatenate([cos, sin], 1)
    return right, left, rows


def dot(a, b):
    return jnp.dot(a, b, preferred_element_type=F32)


def transform_pair(pair, right, left):
    first = dot(pair, right).astype(BF16)
    inner = jnp.concatenate(
        [
            jnp.concatenate([first[:N, :N], first[N:, :N]], 1),
            jnp.concatenate([first[:N, N:], first[N:, N:]], 1),
        ],
        0,
    )
    return dot(left, inner)


def pieces(value):
    high = value.astype(BF16).astype(F32)
    rest = value - high
    mid = rest.astype(BF16).astype(F32)
    return high, mid, rest - mid


def place():
    t = lax.axis_index("tm").astype(I32)
    return t >> 3, t & (C - 1), lax.axis_index("plane").astype(I32)


def own_half():
    _, z, q = place()
    other = (z - q) & (C - 1)
    return jnp.where(other == q, q >> 2, jnp.where(q < other, 1, 0)) * C


def iota(shape, axis):
    return lax.broadcasted_iota(I32, shape, axis)


def deal_kernel(off_in, asg_in, res_in, frames_in, out, frames, off, asg, res, shifted, details, count, sems):
    copies = [
        pltpu.make_async_copy(source, target, sems.at[i])
        for i, (source, target) in enumerate(
            ((off_in, off), (asg_in, asg), (res_in, res), (frames_in, frames))
        )
    ]
    for copy in copies:
        copy.start()
    out[...] = jnp.zeros_like(out)
    details[...] = jnp.zeros_like(details)
    for c in range(C):
        count[c] = 0
    for copy in copies:
        copy.wait()
    for p in range(PD):
        plane = frames[p].astype(F32)
        plane = pltpu.roll(plane, (-off[p, 0]) & (N - 1), 0)
        plane = pltpu.roll(plane, (-off[p, 1]) & (C * N - 1), 1)
        shifted[p] = plane.astype(BF16)
    lane, row = iota((8, N), 1), iota((8, N), 0)
    for p in range(PD):
        for k in range(C):
            c = (asg[p, k] + place()[2]) & (C - 1)
            slot = count[c]
            count[c] = slot + 1
            at = pl.multiple_of(slot * N, N)
            out[c, pl.ds(at, N), :] = shifted[p, :, k * N : (k + 1) * N]
            text = jnp.where(lane == 0, p, 0)
            text = jnp.where(lane == 1, res[p, 0, k], text)
            text = jnp.where(lane == 2, res[p, 1, k], text)
            text = jnp.where(lane == 3, 1, text)
            text = jnp.where(lane == 4, p * C + k, text).astype(F32)
            at = c * (CAP // 2) + slot // 2
            details[at] = jnp.where((row & 1) == (slot & 1), text, details[at])
    for c in range(C):
        for j in range(CAP // 2):
            out[c, CAP * N + 8 * j : CAP * N + 8 * (j + 1), :] = details[
                c * (CAP // 2) + j
            ].astype(BF16)


def tile_kernel(pair, right, left, spec):
    spec[...] = transform_pair(pair[...], right[...], left[...])


def along_of(both, tiles, info, phase):
    outs = []
    for e in range(2):
        p_re, p_im = both[:N, e * N : (e + 1) * N], both[N:, e * N : (e + 1) * N]
        upper = info[e : e + 1, 0:1] > 0.5
        t_re = jnp.where(upper, tiles[:N, N:], tiles[:N, :N])
        t_im = jnp.where(upper, tiles[N:, N:], tiles[N:, :N])
        c_re = p_re * t_re + p_im * t_im
        c_im = p_im * t_re - p_re * t_im
        modulus = jnp.sqrt(c_re * c_re + c_im * c_im)
        level = jnp.sum(jnp.sum(modulus, 0, keepdims=True), 1, keepdims=True) * (1.0 / (N * N))
        scale = 1.0 / (modulus + 0.1 * level + 1e-06)
        n_re = (c_re * scale).astype(BF16)
        n_im = (c_im * scale).astype(BF16)
        lhs = jnp.concatenate([phase[e : e + 1], phase[2 + e : 3 + e]], 0).astype(BF16)
        s_re, s_im = dot(lhs, n_re), dot(lhs, n_im)
        outs.append(
            phase[4 + e : 5 + e] * (s_re[0:1] - s_im[1:2])
            - phase[6 + e : 7 + e] * (s_re[1:2] + s_im[0:1])
        )
    return jnp.concatenate(outs, 0)


def match(spec, tiles, info, phase, along):
    along[...] = jnp.zeros_like(along)

    def one(i, carry):
        along[i, 0:2, :] = along_of(spec[i], tiles[...], info[i], phase[i])
        return carry

    lax.fori_loop(0, PAIRS, one, 0, unroll=16)


def weigh(along, info, w_low, w_high, turn):
    flat = info[...].reshape(C * 16, N)
    row = iota((C * 16, 1), 0)
    live = jnp.where((row & 7) < 2, flat[:, 3:4], 0.0)
    score = jnp.sum(along[...].reshape(C * 16, N), 1, keepdims=True) * (1.0 / N)
    weight = (0.5 + 1.0 / (1.0 + jnp.exp(-score))) * live
    high = weight * flat[:, 0:1]
    low = weight - high
    w_low[...] = jnp.broadcast_to(low, (C * 16, N)).reshape(PAIRS, 8, N)
    w_high[...] = jnp.broadcast_to(high, (C * 16, N)).reshape(PAIRS, 8, N)
    lane = iota((C * 16, N), 1)
    at = flat[:, 4:5].astype(I32) + turn * 16
    table = jnp.where(lane == at, score * live, 0.0).reshape(C, 16, N)
    return jnp.sum(table, 1), jnp.sum(low, 0, keepdims=True), jnp.sum(high, 0, keepdims=True)


def weighted(moved, w_low, w_high, low, high):
    def one(i, carry):
        low, high = carry
        wl, wh = w_low[i], w_high[i]
        for e in range(2):
            patch = moved[2 * i + e].astype(F32)
            low = low + patch * wl[e : e + 1]
            high = high + patch * wh[e : e + 1]
        return low, high

    return lax.fori_loop(0, PAIRS, one, (low, high), unroll=16)


def first_kernel(got, tiles, right, left, rows, msg, spec, moved, phase, info, table, along, w_low, w_high):
    flat = got[:, CAP * N :, :].astype(F32).reshape(C * 16, N)
    row, lane = iota((C * 16, N), 0), iota((C * 16, N), 1)
    info[...] = flat.reshape(PAIRS, 8, N)
    amount = jnp.where((row[:, 0:1] & 7) < 4, flat[:, 1:2], flat[:, 2:3]).astype(I32) & (N - 1)
    wave = dot((lane == amount).astype(BF16), rows[...])
    phase[...] = jnp.where((row & 3) < 2, wave[:, :N], wave[:, N:]).reshape(PAIRS, 8, N)

    def one(i, carry):
        at = pl.multiple_of((i % 2) * 2 * N, 2 * N)
        pair = got[i // 2, pl.ds(at, 2 * N), :]
        both = transform_pair(pair, right[...], left[...])
        spec[i] = both
        text = info[i]
        for e in range(2):
            down = (-text[e, 1].astype(I32)) & (N - 1)
            across = (-text[e, 2].astype(I32)) & (N - 1)
            patch = pltpu.roll(pair[e * N : (e + 1) * N].astype(F32), down, 0)
            moved[2 * i + e] = pltpu.roll(patch, across, 1).astype(BF16)
        return carry

    lax.fori_loop(0, PAIRS, one, 0, unroll=16)
    match(spec, tiles, info, phase, along)
    scores, low_sum, high_sum = weigh(along, info, w_low, w_high, 0)
    table[...] = scores
    zero = jnp.zeros((N, N), F32)
    low, high = weighted(moved, w_low, w_high, zero, zero)
    lines = [jnp.broadcast_to(v, (1, N)) for s in (low_sum, high_sum) for v in pieces(s)]
    tail = jnp.concatenate(lines + [jnp.zeros((2, N), F32)], 0).astype(BF16)
    low, high = low.astype(BF16), high.astype(BF16)
    for b in range(C):
        msg[b, :N, :] = low
        msg[b, N : 2 * N, :] = high
        msg[b, 2 * N :, :] = tail


def second_kernel(got, old, spec, moved, phase, info, table, right, left, msg, tables_out, along, w_low, w_high, tiles):
    total = jnp.zeros((2 * N, N), F32)
    tail = jnp.zeros((8, N), F32)
    for b in range(C):
        total = total + got[b, : 2 * N, :].astype(F32)
        tail = tail + got[b, 2 * N :, :].astype(F32)
    fresh = []
    for p in range(PD):
        count = tail[3 * p : 3 * p + 1] + tail[3 * p + 1 : 3 * p + 2] + tail[3 * p + 2 : 3 * p + 3]
        part = old[p * N : (p + 1) * N, :].astype(F32) + total[p * N : (p + 1) * N]
        fresh.append((part / (1.0 + count)).astype(BF16))
    tiles[...] = transform_pair(jnp.concatenate(fresh, 0), right[...], left[...])
    match(spec, tiles, info, phase, along)
    scores, low_sum, high_sum = weigh(along, info, w_low, w_high, 1)
    tables_out[...] = table[...] + scores
    own = jnp.where(place()[0] == 0, 1.0, 0.0)
    low, high = weighted(
        moved, w_low, w_high, fresh[0].astype(F32) * own, fresh[1].astype(F32) * own
    )
    lines = [
        jnp.broadcast_to(v, (1, N)) for s in (low_sum, high_sum) for v in pieces(s + own)
    ]
    tail = jnp.concatenate(lines + [jnp.zeros((2, N), F32)], 0).astype(BF16)
    low, high = low.astype(BF16), high.astype(BF16)
    msg[...] = jnp.zeros_like(msg)
    half = own_half()
    for b in range(C):
        msg[half + b, :SLAB, :] = low[b * SLAB : (b + 1) * SLAB]
        msg[half + b, SLAB : 2 * SLAB, :] = high[b * SLAB : (b + 1) * SLAB]
        msg[half + b, 2 * SLAB :, :] = tail


def finish_kernel(got, table, msg):
    half = own_half()
    total = got[half].astype(F32)
    for b in range(1, C):
        total = total + got[half + b].astype(F32)
    tail = total[2 * SLAB :]
    slab = []
    for p in range(PD):
        count = tail[3 * p : 3 * p + 1] + tail[3 * p + 1 : 3 * p + 2] + tail[3 * p + 2 : 3 * p + 3]
        slab.append(total[p * SLAB : (p + 1) * SLAB] / count)
    slab = jnp.concatenate(slab, 0).astype(BF16)
    parts = pieces(table[...])
    pad = jnp.zeros((5, N), F32)
    for v in range(C):
        lines = jnp.concatenate([part[v : v + 1] for part in parts] + [pad], 0).astype(BF16)
        for y in range(C):
            msg[y * C + v, : 2 * SLAB, :] = slab
            msg[y * C + v, 2 * SLAB :, :] = lines


def place_kernel(got, out, scores, sems):
    y, _, q = place()
    copies = []
    for z in range(C):
        group = (z - q) & (C - 1)
        for p in range(PD):
            copies.append(
                pltpu.make_async_copy(
                    got.at[:, z, p * SLAB : (p + 1) * SLAB, :],
                    out.at[PD * group + p],
                    sems.at[PD * z + p],
                )
            )
    for copy in copies:
        copy.start()
    total = jnp.zeros((8, N), F32)
    for c in range(C):
        total = total + got[y, c, 2 * SLAB :, :].astype(F32)
    line = total[0:1] + total[1:2] + total[2:3]
    for j in range(2 * PD):
        scores[j // PD, 0, j % PD, :, :] = line[:, j * C : (j + 1) * C]
    for copy in copies:
        copy.wait()


def call(kernel, outs, ins, scratch, args, flops=1e8, grant=16, spread=None):
    spaces = {"s": pltpu.SMEM, "v": pltpu.VMEM, "h": pltpu.HBM}
    size = sum(int(np.prod(o.shape)) * o.dtype.itemsize for o in outs)
    return pl.pallas_call(
        kernel,
        out_shape=outs,
        in_specs=[pl.BlockSpec(memory_space=spaces[i]) for i in ins],
        out_specs=[pl.BlockSpec(memory_space=spaces[o]) for o in spread or "v" * len(outs)],
        scratch_shapes=scratch,
        compiler_params=pltpu.CompilerParams(vmem_limit_bytes=grant << 20),
        cost_estimate=pl.CostEstimate(
            flops=int(flops), bytes_accessed=size + (1 << 20), transcendentals=0
        ),
    )(*args)


def struct(shape, dtype):
    return jax.ShapeDtypeStruct(shape, dtype)


def number(y, z, q):
    return (y * C + z) * C + q


def along_z():
    return [[y * C + z for z in range(C)] for y in range(C)]


def along_y():
    return [[y * C + z for y in range(C)] for z in range(C)]


def across():
    groups = []
    for z in range(C):
        pairs = [(a, (z - a) % C) for a in range(C) if a < (z - a) % C]
        if z % 2 == 0:
            pairs.append((z // 2, z // 2 + C // 2))
        for pair in pairs:
            groups.append([number(y, z, q) for q in pair for y in range(C)])
    return groups


def exchange(value, axis, groups=None):
    return lax.all_to_all(
        value, axis, split_axis=0, concat_axis=0, axis_index_groups=groups, tiled=True
    )


def local(frames, offsets, assign, residual, template):
    right, left, rows = (jnp.asarray(t) for t in tables())
    off = offsets.reshape(PD, 2)
    asg = assign.reshape(PD, C)
    res = residual.reshape(PD, C, 2).transpose(0, 2, 1)
    _, z, q = place()
    other = (z - q) & (C - 1)
    small = (PAIRS, 8, N)
    (dealt,) = call(
        deal_kernel,
        [struct((C, ROWS, N), BF16)],
        "hhhh",
        [
            pltpu.VMEM((PD, N, C * N), BF16),
            pltpu.SMEM((PD, 2), I32),
            pltpu.SMEM((PD, C), I32),
            pltpu.SMEM((PD, 2, C), I32),
            pltpu.VMEM((PD, N, C * N), BF16),
            pltpu.VMEM((C * CAP // 2, 8, N), F32),
            pltpu.SMEM((C,), I32),
            pltpu.SemaphoreType.DMA((4,)),
        ],
        (off, asg, res, frames[0]),
        grant=63,
    )
    got = exchange(dealt, "tm", along_z())
    swap = [
        (number(a, b, c), number(a, b, (b - c) % C))
        for a in range(C)
        for b in range(C)
        for c in range(C)
    ]
    mine = lax.dynamic_slice_in_dim(template, PD * other, PD, 0).reshape(PD * N, N)
    old = lax.ppermute(mine, ("tm", "plane"), swap)
    (tiles,) = call(tile_kernel, [struct((2 * N, 2 * N), F32)], "vvv", [], (old, right, left))
    scratch = [pltpu.VMEM(small, F32) for _ in range(3)]
    msg, spec, moved, phase, info, table = call(
        first_kernel,
        [
            struct((C, 2 * N + 8, N), BF16),
            struct((PAIRS, 2 * N, 2 * N), F32),
            struct((2 * PAIRS, N, N), BF16),
            struct(small, F32),
            struct(small, F32),
            struct((C, N), F32),
        ],
        "vvvvv",
        scratch,
        (got, tiles, right, left, rows),
        flops=1e9,
    )
    got = exchange(msg, "tm", along_y())
    msg, table = call(
        second_kernel,
        [struct((2 * C, 2 * SLAB + 8, N), BF16), struct((C, N), F32)],
        "vvvvvvvvv",
        scratch + [pltpu.VMEM((2 * N, 2 * N), F32)],
        (got, old, spec, moved, phase, info, table, right, left),
        flops=1e9,
    )
    got = exchange(msg, ("tm", "plane"), across())
    (msg,) = call(finish_kernel, [struct((C * C, 2 * SLAB + 8, N), BF16)], "vv", [], (got, table))
    got = exchange(msg, "tm")
    out, scores = call(
        place_kernel,
        [struct((PD * C, C, SLAB, N), BF16), struct((2, 1, PD, 1, C), F32)],
        "v",
        [pltpu.SemaphoreType.DMA((PD * C,))],
        (got.reshape(C, C, 2 * SLAB + 8, N),),
        spread="hv",
    )
    return out.reshape(PD * C, N, N), scores


def solution(mesh):
    return jax.shard_map(
        local,
        mesh=mesh,
        in_specs=(
            P("tm", "plane", None, None),
            P("tm", "plane", None),
            P("tm", "plane", None, None, None),
            P("tm", "plane", None, None, None),
            P(None, None, "plane"),
        ),
        out_specs=(P(None, None, "plane"), P(None, "tm", "plane", None, None)),
        check_vma=False,
    )
```

```python
import jax
import jax.numpy as jnp
import numpy as np
from jax import lax
from jax.experimental import pallas as pl
from jax.experimental.pallas import tpu as pltpu
from jax.sharding import PartitionSpec as P


N = 128
C = 8
PD = 2
CAP = 4
PAIRS = C * CAP // 2
ROWS = CAP * N + 16
SLAB = N // C
F32, BF16, I32 = jnp.float32, jnp.bfloat16, jnp.int32


def tables():
    j = np.arange(N, dtype=np.int32)
    phase = (j[:, None] * j[None, :] % N).astype(np.float32) * np.float32(2.0 * np.pi / N)
    cos = np.cos(phase).astype(BF16)
    sin = np.sin(phase).astype(BF16)
    right = np.concatenate([cos, -sin], 1)
    left = np.concatenate(
        [np.concatenate([cos, sin], 1), np.concatenate([-sin, cos], 1)], 0
    )
    rows = np.concatenate([cos, sin], 1)
    return right, left, rows


def dot(a, b):
    return jnp.dot(a, b, preferred_element_type=F32)


def transform_pair(pair, right, left):
    first = dot(pair, right).astype(BF16)
    inner = jnp.concatenate(
        [
            jnp.concatenate([first[:N, :N], first[N:, :N]], 1),
            jnp.concatenate([first[:N, N:], first[N:, N:]], 1),
        ],
        0,
    )
    return dot(left, inner)


def pieces(value):
    high = value.astype(BF16).astype(F32)
    rest = value - high
    mid = rest.astype(BF16).astype(F32)
    return high, mid, rest - mid


def place():
    t = lax.axis_index("tm").astype(I32)
    return t >> 3, t & (C - 1), lax.axis_index("plane").astype(I32)


def own_half():
    _, z, q = place()
    other = (z - q) & (C - 1)
    return jnp.where(other == q, q >> 2, jnp.where(q < other, 1, 0)) * C


def iota(shape, axis):
    return lax.broadcasted_iota(I32, shape, axis)


def deal_kernel(off_in, asg_in, res_in, frames_in, out, frames, off, asg, res, shifted, details, count, sems):
    copies = [
        pltpu.make_async_copy(source, target, sems.at[i])
        for i, (source, target) in enumerate(
            (
                (off_in, off),
                (asg_in, asg),
                (res_in, res),
                (frames_in.at[0], frames.at[0]),
                (frames_in.at[1], frames.at[1]),
            )
        )
    ]
    for copy in copies:
        copy.start()
    out[...] = jnp.zeros_like(out)
    details[...] = jnp.zeros_like(details)
    for c in range(C):
        count[c] = 0
    for copy in copies[:3]:
        copy.wait()
    for p in range(PD):
        copies[3 + p].wait()
        plane = frames[p].astype(F32)
        plane = pltpu.roll(plane, (-off[p, 0]) & (N - 1), 0)
        plane = pltpu.roll(plane, (-off[p, 1]) & (C * N - 1), 1)
        shifted[p] = plane.astype(BF16)
    lane, row = iota((8, N), 1), iota((8, N), 0)
    for p in range(PD):
        for k in range(C):
            c = (asg[p, k] + place()[2]) & (C - 1)
            slot = count[c]
            count[c] = slot + 1
            at = pl.multiple_of(slot * N, N)
            out[c, pl.ds(at, N), :] = shifted[p, :, k * N : (k + 1) * N]
            text = jnp.where(lane == 0, p, 0)
            text = jnp.where(lane == 1, res[p, 0, k], text)
            text = jnp.where(lane == 2, res[p, 1, k], text)
            text = jnp.where(lane == 3, 1, text)
            text = jnp.where(lane == 4, p * C + k, text).astype(F32)
            at = c * (CAP // 2) + slot // 2
            details[at] = jnp.where((row & 1) == (slot & 1), text, details[at])
    for c in range(C):
        for j in range(CAP // 2):
            out[c, CAP * N + 8 * j : CAP * N + 8 * (j + 1), :] = details[
                c * (CAP // 2) + j
            ].astype(BF16)


def tile_kernel(pair, right, left, spec):
    spec[...] = transform_pair(pair[...], right[...], left[...])


def along_of(both, tiles, info, phase):
    outs = []
    for e in range(2):
        p_re, p_im = both[:N, e * N : (e + 1) * N], both[N:, e * N : (e + 1) * N]
        upper = info[e : e + 1, 0:1] > 0.5
        t_re = jnp.where(upper, tiles[:N, N:], tiles[:N, :N])
        t_im = jnp.where(upper, tiles[N:, N:], tiles[N:, :N])
        c_re = p_re * t_re + p_im * t_im
        c_im = p_im * t_re - p_re * t_im
        modulus = jnp.sqrt(c_re * c_re + c_im * c_im)
        level = jnp.sum(jnp.sum(modulus, 0, keepdims=True), 1, keepdims=True) * (1.0 / (N * N))
        scale = 1.0 / (modulus + (0.1 * level + 1e-06))
        n_re = (c_re * scale).astype(BF16)
        n_im = (c_im * scale).astype(BF16)
        lhs = jnp.concatenate([phase[e : e + 1], phase[2 + e : 3 + e]], 0).astype(BF16)
        s_re, s_im = dot(lhs, n_re), dot(lhs, n_im)
        outs.append(
            phase[4 + e : 5 + e] * (s_re[0:1] - s_im[1:2])
            - phase[6 + e : 7 + e] * (s_re[1:2] + s_im[0:1])
        )
    return jnp.concatenate(outs, 0)


def match(spec, tiles, info, phase, along):
    along[...] = jnp.zeros_like(along)

    def one(i, carry):
        along[i, 0:2, :] = along_of(spec[i], tiles[...], info[i], phase[i])
        return carry

    lax.fori_loop(0, PAIRS, one, 0, unroll=16)


def weigh(along, info, w_low, w_high, turn):
    flat = info[...].reshape(C * 16, N)
    row = iota((C * 16, 1), 0)
    live = jnp.where((row & 7) < 2, flat[:, 3:4], 0.0)
    score = jnp.sum(along[...].reshape(C * 16, N), 1, keepdims=True) * (1.0 / N)
    weight = (0.5 + 1.0 / (1.0 + jnp.exp(-score))) * live
    high = weight * flat[:, 0:1]
    low = weight - high
    w_low[...] = jnp.broadcast_to(low, (C * 16, N)).reshape(PAIRS, 8, N)
    w_high[...] = jnp.broadcast_to(high, (C * 16, N)).reshape(PAIRS, 8, N)
    lane = iota((C * 16, N), 1)
    at = flat[:, 4:5].astype(I32) + turn * 16
    table = jnp.where(lane == at, score * live, 0.0).reshape(C, 16, N)
    return jnp.sum(table, 1), jnp.sum(low, 0, keepdims=True), jnp.sum(high, 0, keepdims=True)


def weighted(moved, w_low, w_high, low, high):
    def one(i, carry):
        low, high = carry
        wl, wh = w_low[i], w_high[i]
        for e in range(2):
            patch = moved[2 * i + e].astype(F32)
            low = low + patch * wl[e : e + 1]
            high = high + patch * wh[e : e + 1]
        return low, high

    return lax.fori_loop(0, PAIRS, one, (low, high), unroll=16)


def first_kernel(got, tiles, right, left, rows, msg, spec, moved, phase, info, table, along, w_low, w_high):
    flat = got[:, CAP * N :, :].astype(F32).reshape(C * 16, N)
    row, lane = iota((C * 16, N), 0), iota((C * 16, N), 1)
    info[...] = flat.reshape(PAIRS, 8, N)
    amount = jnp.where((row[:, 0:1] & 7) < 4, flat[:, 1:2], flat[:, 2:3]).astype(I32) & (N - 1)
    wave = dot((lane == amount).astype(BF16), rows[...])
    phase[...] = jnp.where((row & 3) < 2, wave[:, :N], wave[:, N:]).reshape(PAIRS, 8, N)

    def one(i, carry):
        at = pl.multiple_of((i % 2) * 2 * N, 2 * N)
        pair = got[i // 2, pl.ds(at, 2 * N), :]
        both = transform_pair(pair, right[...], left[...])
        spec[i] = both
        text = info[i]
        for e in range(2):
            down = (-text[e, 1].astype(I32)) & (N - 1)
            across = (-text[e, 2].astype(I32)) & (N - 1)
            patch = pltpu.roll(pair[e * N : (e + 1) * N].astype(F32), down, 0)
            moved[2 * i + e] = pltpu.roll(patch, across, 1).astype(BF16)
        return carry

    lax.fori_loop(0, PAIRS, one, 0, unroll=16)
    match(spec, tiles, info, phase, along)
    scores, low_sum, high_sum = weigh(along, info, w_low, w_high, 0)
    table[...] = scores
    zero = jnp.zeros((N, N), F32)
    low, high = weighted(moved, w_low, w_high, zero, zero)
    lines = [jnp.broadcast_to(v, (1, N)) for s in (low_sum, high_sum) for v in pieces(s)]
    tail = jnp.concatenate(lines + [jnp.zeros((2, N), F32)], 0).astype(BF16)
    low, high = low.astype(BF16), high.astype(BF16)
    for b in range(C):
        msg[b, :N, :] = low
        msg[b, N : 2 * N, :] = high
        msg[b, 2 * N :, :] = tail


def second_kernel(got, old, spec, moved, phase, info, table, right, left, msg, tables_out, along, w_low, w_high, tiles):
    total = jnp.zeros((2 * N, N), F32)
    tail = jnp.zeros((8, N), F32)
    for b in range(C):
        total = total + got[b, : 2 * N, :].astype(F32)
        tail = tail + got[b, 2 * N :, :].astype(F32)
    fresh = []
    for p in range(PD):
        count = tail[3 * p : 3 * p + 1] + tail[3 * p + 1 : 3 * p + 2] + tail[3 * p + 2 : 3 * p + 3]
        part = old[p * N : (p + 1) * N, :].astype(F32) + total[p * N : (p + 1) * N]
        fresh.append((part / (1.0 + count)).astype(BF16))
    tiles[...] = transform_pair(jnp.concatenate(fresh, 0), right[...], left[...])
    match(spec, tiles, info, phase, along)
    scores, low_sum, high_sum = weigh(along, info, w_low, w_high, 1)
    tables_out[...] = table[...] + scores
    own = jnp.where(place()[0] == 0, 1.0, 0.0)
    low, high = weighted(
        moved, w_low, w_high, fresh[0].astype(F32) * own, fresh[1].astype(F32) * own
    )
    lines = [
        jnp.broadcast_to(v, (1, N)) for s in (low_sum, high_sum) for v in pieces(s + own)
    ]
    tail = jnp.concatenate(lines + [jnp.zeros((2, N), F32)], 0).astype(BF16)
    low, high = low.astype(BF16), high.astype(BF16)
    msg[...] = jnp.zeros_like(msg)
    half = own_half()
    for b in range(C):
        msg[half + b, :SLAB, :] = low[b * SLAB : (b + 1) * SLAB]
        msg[half + b, SLAB : 2 * SLAB, :] = high[b * SLAB : (b + 1) * SLAB]
        msg[half + b, 2 * SLAB :, :] = tail


def finish_kernel(got, table, msg):
    half = own_half()
    total = got[half].astype(F32)
    for b in range(1, C):
        total = total + got[half + b].astype(F32)
    tail = total[2 * SLAB :]
    slab = []
    for p in range(PD):
        count = tail[3 * p : 3 * p + 1] + tail[3 * p + 1 : 3 * p + 2] + tail[3 * p + 2 : 3 * p + 3]
        slab.append(total[p * SLAB : (p + 1) * SLAB] / count)
    slab = jnp.concatenate(slab, 0).astype(BF16)
    parts = pieces(table[...])
    pad = jnp.zeros((5, N), F32)
    for v in range(C):
        lines = jnp.concatenate([part[v : v + 1] for part in parts] + [pad], 0).astype(BF16)
        for y in range(C):
            msg[y * C + v, : 2 * SLAB, :] = slab
            msg[y * C + v, 2 * SLAB :, :] = lines


def place_kernel(got, out, scores, tiles, sems):
    y, _, q = place()
    copies = []
    for z in range(C):
        group = (z - q) & (C - 1)
        for b in range(C):
            for p in range(PD):
                tiles[z, p, b] = got[b, z, p * SLAB : (p + 1) * SLAB, :]
        copy = pltpu.make_async_copy(tiles.at[z], out.at[group], sems.at[z])
        copy.start()
        copies.append(copy)
    total = jnp.zeros((8, N), F32)
    for c in range(C):
        total = total + got[y, c, 2 * SLAB :, :].astype(F32)
    line = total[0:1] + total[1:2] + total[2:3]
    for j in range(2 * PD):
        scores[j // PD, 0, j % PD, :, :] = line[:, j * C : (j + 1) * C]
    for copy in copies:
        copy.wait()


def call(kernel, outs, ins, scratch, args, flops=1e8, grant=16, spread=None):
    spaces = {"s": pltpu.SMEM, "v": pltpu.VMEM, "h": pltpu.HBM}
    size = sum(int(np.prod(o.shape)) * o.dtype.itemsize for o in outs)
    return pl.pallas_call(
        kernel,
        out_shape=outs,
        in_specs=[pl.BlockSpec(memory_space=spaces[i]) for i in ins],
        out_specs=[pl.BlockSpec(memory_space=spaces[o]) for o in spread or "v" * len(outs)],
        scratch_shapes=scratch,
        compiler_params=pltpu.CompilerParams(vmem_limit_bytes=grant << 20),
        cost_estimate=pl.CostEstimate(
            flops=int(flops), bytes_accessed=size + (1 << 20), transcendentals=0
        ),
    )(*args)


def struct(shape, dtype):
    return jax.ShapeDtypeStruct(shape, dtype)


def number(y, z, q):
    return (y * C + z) * C + q


def along_z():
    return [[y * C + z for z in range(C)] for y in range(C)]


def along_y():
    return [[y * C + z for y in range(C)] for z in range(C)]


def across():
    groups = []
    for z in range(C):
        pairs = [(a, (z - a) % C) for a in range(C) if a < (z - a) % C]
        if z % 2 == 0:
            pairs.append((z // 2, z // 2 + C // 2))
        for pair in pairs:
            groups.append([number(y, z, q) for q in pair for y in range(C)])
    return groups


def exchange(value, axis, groups=None):
    return lax.all_to_all(
        value, axis, split_axis=0, concat_axis=0, axis_index_groups=groups, tiled=True
    )


def local(frames, offsets, assign, residual, template):
    right, left, rows = (jnp.asarray(t) for t in tables())
    off = offsets.reshape(PD, 2)
    asg = assign.reshape(PD, C)
    res = residual.reshape(PD, C, 2).transpose(0, 2, 1)
    _, z, q = place()
    other = (z - q) & (C - 1)
    small = (PAIRS, 8, N)
    (dealt,) = call(
        deal_kernel,
        [struct((C, ROWS, N), BF16)],
        "hhhh",
        [
            pltpu.VMEM((PD, N, C * N), BF16),
            pltpu.SMEM((PD, 2), I32),
            pltpu.SMEM((PD, C), I32),
            pltpu.SMEM((PD, 2, C), I32),
            pltpu.VMEM((PD, N, C * N), BF16),
            pltpu.VMEM((C * CAP // 2, 8, N), F32),
            pltpu.SMEM((C,), I32),
            pltpu.SemaphoreType.DMA((5,)),
        ],
        (off, asg, res, frames[0]),
        grant=63,
    )
    got = exchange(dealt, "tm", along_z())
    swap = [
        (number(a, b, c), number(a, b, (b - c) % C))
        for a in range(C)
        for b in range(C)
        for c in range(C)
    ]
    mine = lax.dynamic_slice_in_dim(template, PD * other, PD, 0).reshape(PD * N, N)
    old = lax.ppermute(mine, ("tm", "plane"), swap)
    (tiles,) = call(tile_kernel, [struct((2 * N, 2 * N), F32)], "vvv", [], (old, right, left))
    scratch = [pltpu.VMEM(small, F32) for _ in range(3)]
    msg, spec, moved, phase, info, table = call(
        first_kernel,
        [
            struct((C, 2 * N + 8, N), BF16),
            struct((PAIRS, 2 * N, 2 * N), F32),
            struct((2 * PAIRS, N, N), BF16),
            struct(small, F32),
            struct(small, F32),
            struct((C, N), F32),
        ],
        "vvvvv",
        scratch,
        (got, tiles, right, left, rows),
        flops=1e9,
    )
    got = exchange(msg, "tm", along_y())
    msg, table = call(
        second_kernel,
        [struct((2 * C, 2 * SLAB + 8, N), BF16), struct((C, N), F32)],
        "vvvvvvvvv",
        scratch + [pltpu.VMEM((2 * N, 2 * N), F32)],
        (got, old, spec, moved, phase, info, table, right, left),
        flops=1e9,
    )
    got = exchange(msg, ("tm", "plane"), across())
    (msg,) = call(finish_kernel, [struct((C * C, 2 * SLAB + 8, N), BF16)], "vv", [], (got, table))
    got = exchange(msg, "tm")
    out, scores = call(
        place_kernel,
        [struct((C, PD, C, SLAB, N), BF16), struct((2, 1, PD, 1, C), F32)],
        "v",
        [pltpu.VMEM((C, PD, C, SLAB, N), BF16), pltpu.SemaphoreType.DMA((C,))],
        (got.reshape(C, C, 2 * SLAB + 8, N),),
        spread="hv",
    )
    return out.reshape(PD * C, N, N), scores


def solution(mesh):
    return jax.shard_map(
        local,
        mesh=mesh,
        in_specs=(
            P("tm", "plane", None, None),
            P("tm", "plane", None),
            P("tm", "plane", None, None, None),
            P("tm", "plane", None, None, None),
            P(None, None, "plane"),
        ),
        out_specs=(P(None, None, "plane"), P(None, "tm", "plane", None, None)),
        check_vma=False,
    )
```

```python
import jax
import jax.numpy as jnp
import numpy as np
from jax import lax
from jax.experimental import pallas as pl
from jax.experimental.pallas import tpu as pltpu
from jax.sharding import PartitionSpec as P


N = 128
C = 8
PD = 2
CAP = 4
PAIRS = C * CAP // 2
ROWS = CAP * N + 16
SLAB = N // C
F32, BF16, I32 = jnp.float32, jnp.bfloat16, jnp.int32


def tables():
    j = np.arange(N, dtype=np.int32)
    phase = (j[:, None] * j[None, :] % N).astype(np.float32) * np.float32(2.0 * np.pi / N)
    cos = np.cos(phase).astype(BF16)
    sin = np.sin(phase).astype(BF16)
    right = np.concatenate([cos, -sin], 1)
    left = np.concatenate(
        [np.concatenate([cos, sin], 1), np.concatenate([-sin, cos], 1)], 0
    )
    rows = np.concatenate([cos, sin], 1)
    return right, left, rows


def dot(a, b):
    return jnp.dot(a, b, preferred_element_type=F32)


def transform_pair(pair, right, left):
    first = dot(pair, right).astype(BF16)
    inner = jnp.concatenate(
        [
            jnp.concatenate([first[:N, :N], first[N:, :N]], 1),
            jnp.concatenate([first[:N, N:], first[N:, N:]], 1),
        ],
        0,
    )
    return dot(left, inner)


def pieces(value):
    high = value.astype(BF16).astype(F32)
    rest = value - high
    mid = rest.astype(BF16).astype(F32)
    return high, mid, rest - mid


def place():
    t = lax.axis_index("tm").astype(I32)
    return t >> 3, t & (C - 1), lax.axis_index("plane").astype(I32)


def own_half():
    _, z, q = place()
    other = (z - q) & (C - 1)
    return jnp.where(other == q, q >> 2, jnp.where(q < other, 1, 0)) * C


def iota(shape, axis):
    return lax.broadcasted_iota(I32, shape, axis)


def deal_kernel(off_in, asg_in, res_in, frames_in, out, frames, off, asg, res, shifted, details, count, sems):
    copies = [
        pltpu.make_async_copy(source, target, sems.at[i])
        for i, (source, target) in enumerate(
            ((off_in, off), (asg_in, asg), (res_in, res), (frames_in, frames))
        )
    ]
    for copy in copies:
        copy.start()
    out[...] = jnp.zeros_like(out)
    details[...] = jnp.zeros_like(details)
    for c in range(C):
        count[c] = 0
    for copy in copies:
        copy.wait()
    for p in range(PD):
        plane = frames[p].astype(F32)
        plane = pltpu.roll(plane, (-off[p, 0]) & (N - 1), 0)
        plane = pltpu.roll(plane, (-off[p, 1]) & (C * N - 1), 1)
        shifted[p] = plane.astype(BF16)
    lane, row = iota((8, N), 1), iota((8, N), 0)
    for p in range(PD):
        for k in range(C):
            c = (asg[p, k] + place()[2]) & (C - 1)
            slot = count[c]
            count[c] = slot + 1
            at = pl.multiple_of(slot * N, N)
            out[c, pl.ds(at, N), :] = shifted[p, :, k * N : (k + 1) * N]
            text = jnp.where(lane == 0, p, 0)
            text = jnp.where(lane == 1, res[p, 0, k], text)
            text = jnp.where(lane == 2, res[p, 1, k], text)
            text = jnp.where(lane == 3, 1, text)
            text = jnp.where(lane == 4, p * C + k, text).astype(F32)
            at = c * (CAP // 2) + slot // 2
            details[at] = jnp.where((row & 1) == (slot & 1), text, details[at])
    for c in range(C):
        for j in range(CAP // 2):
            out[c, CAP * N + 8 * j : CAP * N + 8 * (j + 1), :] = details[
                c * (CAP // 2) + j
            ].astype(BF16)


def tile_kernel(pair, right, left, spec):
    spec[...] = transform_pair(pair[...], right[...], left[...])


def along_of(both, tiles, info, phase):
    outs = []
    for e in range(2):
        p_re, p_im = both[:N, e * N : (e + 1) * N], both[N:, e * N : (e + 1) * N]
        upper = info[e : e + 1, 0:1] > 0.5
        t_re = jnp.where(upper, tiles[:N, N:], tiles[:N, :N])
        t_im = jnp.where(upper, tiles[N:, N:], tiles[N:, :N])
        c_re = p_re * t_re + p_im * t_im
        c_im = p_im * t_re - p_re * t_im
        modulus = jnp.sqrt(c_re * c_re + c_im * c_im)
        level = jnp.sum(jnp.sum(modulus, 0, keepdims=True), 1, keepdims=True) * (1.0 / (N * N))
        scale = 1.0 / (modulus + 0.1 * level + 1e-06)
        n_re = (c_re * scale).astype(BF16)
        n_im = (c_im * scale).astype(BF16)
        lhs = jnp.concatenate([phase[e : e + 1], phase[2 + e : 3 + e]], 0).astype(BF16)
        s_re, s_im = dot(lhs, n_re), dot(lhs, n_im)
        outs.append(
            phase[4 + e : 5 + e] * (s_re[0:1] - s_im[1:2])
            - phase[6 + e : 7 + e] * (s_re[1:2] + s_im[0:1])
        )
    return jnp.concatenate(outs, 0)


def match(spec, tiles, info, phase, along):
    along[...] = jnp.zeros_like(along)

    def one(i, carry):
        along[i, 0:2, :] = along_of(spec[i], tiles[...], info[i], phase[i])
        return carry

    lax.fori_loop(0, PAIRS, one, 0, unroll=16)


def weigh(along, info, w_low, w_high, turn):
    flat = info[...].reshape(C * 16, N)
    row = iota((C * 16, 1), 0)
    live = jnp.where((row & 7) < 2, flat[:, 3:4], 0.0)
    score = jnp.sum(along[...].reshape(C * 16, N), 1, keepdims=True) * (1.0 / N)
    weight = (0.5 + 1.0 / (1.0 + jnp.exp(-score))) * live
    high = weight * flat[:, 0:1]
    low = weight - high
    w_low[...] = jnp.broadcast_to(low, (C * 16, N)).reshape(PAIRS, 8, N)
    w_high[...] = jnp.broadcast_to(high, (C * 16, N)).reshape(PAIRS, 8, N)
    lane = iota((C * 16, N), 1)
    at = flat[:, 4:5].astype(I32) + turn * 16
    table = jnp.where(lane == at, score * live, 0.0).reshape(C, 16, N)
    return jnp.sum(table, 1), jnp.sum(low, 0, keepdims=True), jnp.sum(high, 0, keepdims=True)


def weighted(moved, w_low, w_high, low, high):
    def one(i, carry):
        low, high = carry
        wl, wh = w_low[i], w_high[i]
        for e in range(2):
            patch = moved[2 * i + e].astype(F32)
            low = low + patch * wl[e : e + 1]
            high = high + patch * wh[e : e + 1]
        return low, high

    return lax.fori_loop(0, PAIRS, one, (low, high), unroll=16)


def first_kernel(got, tiles, right, left, rows, msg, spec, moved, phase, info, table, along, w_low, w_high):
    flat = got[:, CAP * N :, :].astype(F32).reshape(C * 16, N)
    row, lane = iota((C * 16, N), 0), iota((C * 16, N), 1)
    info[...] = flat.reshape(PAIRS, 8, N)
    amount = jnp.where((row[:, 0:1] & 7) < 4, flat[:, 1:2], flat[:, 2:3]).astype(I32) & (N - 1)
    wave = dot((lane == amount).astype(BF16), rows[...])
    phase[...] = jnp.where((row & 3) < 2, wave[:, :N], wave[:, N:]).reshape(PAIRS, 8, N)

    def one(i, carry):
        at = pl.multiple_of((i % 2) * 2 * N, 2 * N)
        pair = got[i // 2, pl.ds(at, 2 * N), :]
        both = transform_pair(pair, right[...], left[...])
        spec[i] = both
        text = info[i]
        for e in range(2):
            down = (-text[e, 1].astype(I32)) & (N - 1)
            across = (-text[e, 2].astype(I32)) & (N - 1)
            patch = pltpu.roll(pair[e * N : (e + 1) * N].astype(F32), down, 0)
            moved[2 * i + e] = pltpu.roll(patch, across, 1).astype(BF16)
        return carry

    lax.fori_loop(0, PAIRS, one, 0, unroll=16)
    match(spec, tiles, info, phase, along)
    scores, low_sum, high_sum = weigh(along, info, w_low, w_high, 0)
    table[...] = scores
    zero = jnp.zeros((N, N), F32)
    low, high = weighted(moved, w_low, w_high, zero, zero)
    lines = [jnp.broadcast_to(v, (1, N)) for s in (low_sum, high_sum) for v in pieces(s)]
    tail = jnp.concatenate(lines + [jnp.zeros((2, N), F32)], 0).astype(BF16)
    low, high = low.astype(BF16), high.astype(BF16)
    for b in range(C):
        msg[b, :N, :] = low
        msg[b, N : 2 * N, :] = high
        msg[b, 2 * N :, :] = tail


def second_kernel(got, old, spec, moved, phase, info, table, right, left, msg, tables_out, along, w_low, w_high, tiles):
    total = jnp.zeros((2 * N, N), F32)
    tail = jnp.zeros((8, N), F32)
    for b in range(C):
        total = total + got[b, : 2 * N, :].astype(F32)
        tail = tail + got[b, 2 * N :, :].astype(F32)
    fresh = []
    for p in range(PD):
        count = tail[3 * p : 3 * p + 1] + tail[3 * p + 1 : 3 * p + 2] + tail[3 * p + 2 : 3 * p + 3]
        part = old[p * N : (p + 1) * N, :].astype(F32) + total[p * N : (p + 1) * N]
        fresh.append((part / (1.0 + count)).astype(BF16))
    tiles[...] = transform_pair(jnp.concatenate(fresh, 0), right[...], left[...])
    match(spec, tiles, info, phase, along)
    scores, low_sum, high_sum = weigh(along, info, w_low, w_high, 1)
    tables_out[...] = table[...] + scores
    own = jnp.where(place()[0] == 0, 1.0, 0.0)
    low, high = weighted(
        moved, w_low, w_high, fresh[0].astype(F32) * own, fresh[1].astype(F32) * own
    )
    lines = [jnp.broadcast_to(s + own, (1, N)) for s in (low_sum, high_sum)]
    tail = jnp.concatenate(lines + [jnp.zeros((6, N), F32)], 0)
    msg[...] = jnp.zeros_like(msg)
    half = own_half()
    for b in range(C):
        msg[half + b, :SLAB, :] = low[b * SLAB : (b + 1) * SLAB]
        msg[half + b, SLAB : 2 * SLAB, :] = high[b * SLAB : (b + 1) * SLAB]
        msg[half + b, 2 * SLAB :, :] = tail


def finish_kernel(got, table, msg):
    half = own_half()
    total = got[half]
    for b in range(1, C):
        total = total + got[half + b]
    slab = []
    for p in range(PD):
        count = total[2 * SLAB + p : 2 * SLAB + p + 1]
        slab.append(total[p * SLAB : (p + 1) * SLAB] / count)
    slab = jnp.concatenate(slab, 0).astype(BF16)
    parts = pieces(table[...])
    pad = jnp.zeros((5, N), F32)
    for v in range(C):
        lines = jnp.concatenate([part[v : v + 1] for part in parts] + [pad], 0).astype(BF16)
        for y in range(C):
            msg[y * C + v, : 2 * SLAB, :] = slab
            msg[y * C + v, 2 * SLAB :, :] = lines


def place_kernel(got, out, scores, sems):
    y, _, q = place()
    copies = []
    for z in range(C):
        group = (z - q) & (C - 1)
        for p in range(PD):
            copies.append(
                pltpu.make_async_copy(
                    got.at[:, z, p * SLAB : (p + 1) * SLAB, :],
                    out.at[PD * group + p],
                    sems.at[PD * z + p],
                )
            )
    for copy in copies:
        copy.start()
    total = jnp.zeros((8, N), F32)
    for c in range(C):
        total = total + got[y, c, 2 * SLAB :, :].astype(F32)
    line = total[0:1] + total[1:2] + total[2:3]
    for j in range(2 * PD):
        scores[j // PD, 0, j % PD, :, :] = line[:, j * C : (j + 1) * C]
    for copy in copies:
        copy.wait()


def call(kernel, outs, ins, scratch, args, flops=1e8, grant=16, spread=None):
    spaces = {"s": pltpu.SMEM, "v": pltpu.VMEM, "h": pltpu.HBM}
    size = sum(int(np.prod(o.shape)) * o.dtype.itemsize for o in outs)
    return pl.pallas_call(
        kernel,
        out_shape=outs,
        in_specs=[pl.BlockSpec(memory_space=spaces[i]) for i in ins],
        out_specs=[pl.BlockSpec(memory_space=spaces[o]) for o in spread or "v" * len(outs)],
        scratch_shapes=scratch,
        compiler_params=pltpu.CompilerParams(vmem_limit_bytes=grant << 20),
        cost_estimate=pl.CostEstimate(
            flops=int(flops), bytes_accessed=size + (1 << 20), transcendentals=0
        ),
    )(*args)


def struct(shape, dtype):
    return jax.ShapeDtypeStruct(shape, dtype)


def number(y, z, q):
    return (y * C + z) * C + q


def along_z():
    return [[y * C + z for z in range(C)] for y in range(C)]


def along_y():
    return [[y * C + z for y in range(C)] for z in range(C)]


def across():
    groups = []
    for z in range(C):
        pairs = [(a, (z - a) % C) for a in range(C) if a < (z - a) % C]
        if z % 2 == 0:
            pairs.append((z // 2, z // 2 + C // 2))
        for pair in pairs:
            groups.append([number(y, z, q) for q in pair for y in range(C)])
    return groups


def exchange(value, axis, groups=None):
    return lax.all_to_all(
        value, axis, split_axis=0, concat_axis=0, axis_index_groups=groups, tiled=True
    )


def local(frames, offsets, assign, residual, template):
    right, left, rows = (jnp.asarray(t) for t in tables())
    off = offsets.reshape(PD, 2)
    asg = assign.reshape(PD, C)
    res = residual.reshape(PD, C, 2).transpose(0, 2, 1)
    _, z, q = place()
    other = (z - q) & (C - 1)
    small = (PAIRS, 8, N)
    (dealt,) = call(
        deal_kernel,
        [struct((C, ROWS, N), BF16)],
        "hhhh",
        [
            pltpu.VMEM((PD, N, C * N), BF16),
            pltpu.SMEM((PD, 2), I32),
            pltpu.SMEM((PD, C), I32),
            pltpu.SMEM((PD, 2, C), I32),
            pltpu.VMEM((PD, N, C * N), BF16),
            pltpu.VMEM((C * CAP // 2, 8, N), F32),
            pltpu.SMEM((C,), I32),
            pltpu.SemaphoreType.DMA((4,)),
        ],
        (off, asg, res, frames[0]),
        grant=63,
    )
    got = exchange(dealt, "tm", along_z())
    swap = [
        (number(a, b, c), number(a, b, (b - c) % C))
        for a in range(C)
        for b in range(C)
        for c in range(C)
    ]
    mine = lax.dynamic_slice_in_dim(template, PD * other, PD, 0).reshape(PD * N, N)
    old = lax.ppermute(mine, ("tm", "plane"), swap)
    (tiles,) = call(tile_kernel, [struct((2 * N, 2 * N), F32)], "vvv", [], (old, right, left))
    scratch = [pltpu.VMEM(small, F32) for _ in range(3)]
    msg, spec, moved, phase, info, table = call(
        first_kernel,
        [
            struct((C, 2 * N + 8, N), BF16),
            struct((PAIRS, 2 * N, 2 * N), F32),
            struct((2 * PAIRS, N, N), BF16),
            struct(small, F32),
            struct(small, F32),
            struct((C, N), F32),
        ],
        "vvvvv",
        scratch,
        (got, tiles, right, left, rows),
        flops=1e9,
    )
    got = exchange(msg, "tm", along_y())
    msg, table = call(
        second_kernel,
        [struct((2 * C, 2 * SLAB + 8, N), F32), struct((C, N), F32)],
        "vvvvvvvvv",
        scratch + [pltpu.VMEM((2 * N, 2 * N), F32)],
        (got, old, spec, moved, phase, info, table, right, left),
        flops=1e9,
    )
    got = exchange(msg, ("tm", "plane"), across())
    (msg,) = call(finish_kernel, [struct((C * C, 2 * SLAB + 8, N), BF16)], "vv", [], (got, table))
    got = exchange(msg, "tm")
    out, scores = call(
        place_kernel,
        [struct((PD * C, C, SLAB, N), BF16), struct((2, 1, PD, 1, C), F32)],
        "v",
        [pltpu.SemaphoreType.DMA((PD * C,))],
        (got.reshape(C, C, 2 * SLAB + 8, N),),
        spread="hv",
    )
    return out.reshape(PD * C, N, N), scores


def solution(mesh):
    return jax.shard_map(
        local,
        mesh=mesh,
        in_specs=(
            P("tm", "plane", None, None),
            P("tm", "plane", None),
            P("tm", "plane", None, None, None),
            P("tm", "plane", None, None, None),
            P(None, None, "plane"),
        ),
        out_specs=(P(None, None, "plane"), P(None, "tm", "plane", None, None)),
        check_vma=False,
    )
```

```python
import jax
import jax.numpy as jnp
import numpy as np
from jax import lax
from jax.experimental import pallas as pl
from jax.experimental.pallas import tpu as pltpu
from jax.sharding import PartitionSpec as P


N = 128
C = 8
PD = 2
CAP = 4
PAIRS = C * CAP // 2
ROWS = CAP * N + 16
SLAB = N // C
F32, BF16, I32 = jnp.float32, jnp.bfloat16, jnp.int32


def tables():
    j = np.arange(N, dtype=np.int32)
    phase = (j[:, None] * j[None, :] % N).astype(np.float32) * np.float32(2.0 * np.pi / N)
    cos = np.cos(phase).astype(BF16)
    sin = np.sin(phase).astype(BF16)
    right = np.concatenate([cos, -sin], 1)
    left = np.concatenate(
        [np.concatenate([cos, sin], 1), np.concatenate([-sin, cos], 1)], 0
    )
    rows = np.concatenate([cos, sin], 1)
    return right, left, rows


def dot(a, b):
    return jnp.dot(a, b, preferred_element_type=F32)


def transform_pair(pair, right, left):
    first = dot(pair, right).astype(BF16)
    inner = jnp.concatenate(
        [
            jnp.concatenate([first[:N, :N], first[N:, :N]], 1),
            jnp.concatenate([first[:N, N:], first[N:, N:]], 1),
        ],
        0,
    )
    return dot(left, inner)


def pieces(value):
    high = value.astype(BF16).astype(F32)
    rest = value - high
    mid = rest.astype(BF16).astype(F32)
    return high, mid, rest - mid


def place():
    t = lax.axis_index("tm").astype(I32)
    return t >> 3, t & (C - 1), lax.axis_index("plane").astype(I32)


def own_half():
    _, z, q = place()
    other = (z - q) & (C - 1)
    return jnp.where(other == q, q >> 2, jnp.where(q < other, 1, 0)) * C


def iota(shape, axis):
    return lax.broadcasted_iota(I32, shape, axis)


def deal_kernel(off_in, asg_in, res_in, frames_in, out, frames, off, asg, res, shifted, details, count, sems):
    copies = [
        pltpu.make_async_copy(source, target, sems.at[i])
        for i, (source, target) in enumerate(
            ((off_in, off), (asg_in, asg), (res_in, res), (frames_in, frames))
        )
    ]
    for copy in copies:
        copy.start()
    out[...] = jnp.zeros_like(out)
    details[...] = jnp.zeros_like(details)
    for c in range(C):
        count[c] = 0
    for copy in copies:
        copy.wait()
    for p in range(PD):
        plane = frames[p].astype(F32)
        plane = pltpu.roll(plane, (-off[p, 0]) & (N - 1), 0)
        plane = pltpu.roll(plane, (-off[p, 1]) & (C * N - 1), 1)
        shifted[p] = plane.astype(BF16)
    lane, row = iota((8, N), 1), iota((8, N), 0)
    for p in range(PD):
        for k in range(C):
            c = (asg[p, k] + place()[2]) & (C - 1)
            slot = count[c]
            count[c] = slot + 1
            at = pl.multiple_of(slot * N, N)
            out[c, pl.ds(at, N), :] = shifted[p, :, k * N : (k + 1) * N]
            text = jnp.where(lane == 0, p, 0)
            text = jnp.where(lane == 1, res[p, 0, k], text)
            text = jnp.where(lane == 2, res[p, 1, k], text)
            text = jnp.where(lane == 3, 1, text)
            text = jnp.where(lane == 4, p * C + k, text).astype(F32)
            at = c * (CAP // 2) + slot // 2
            details[at] = jnp.where((row & 1) == (slot & 1), text, details[at])
    for c in range(C):
        for j in range(CAP // 2):
            out[c, CAP * N + 8 * j : CAP * N + 8 * (j + 1), :] = details[
                c * (CAP // 2) + j
            ].astype(BF16)


def tile_kernel(pair, right, left, spec):
    spec[...] = transform_pair(pair[...], right[...], left[...])


def along_of(both, tiles, info, phase):
    parts = []
    for e in range(2):
        p_re, p_im = both[:N, e * N : (e + 1) * N], both[N:, e * N : (e + 1) * N]
        upper = info[e : e + 1, 0:1] > 0.5
        t_re = jnp.where(upper, tiles[:N, N:], tiles[:N, :N])
        t_im = jnp.where(upper, tiles[N:, N:], tiles[N:, :N])
        c_re = p_re * t_re + p_im * t_im
        c_im = p_im * t_re - p_re * t_im
        modulus = jnp.sqrt(c_re * c_re + c_im * c_im)
        level = jnp.sum(jnp.sum(modulus, 0, keepdims=True), 1, keepdims=True) * (1.0 / (N * N))
        scale = 1.0 / (modulus + 0.1 * level + 1e-06)
        parts.append(((c_re * scale).astype(BF16), (c_im * scale).astype(BF16)))
    lhs = phase[0:4].astype(BF16)
    s_re = dot(lhs, jnp.concatenate([parts[0][0], parts[1][0]], 1))
    s_im = dot(lhs, jnp.concatenate([parts[0][1], parts[1][1]], 1))
    outs = []
    for e in range(2):
        at = slice(e * N, (e + 1) * N)
        outs.append(
            phase[4 + e : 5 + e] * (s_re[e : e + 1, at] - s_im[2 + e : 3 + e, at])
            - phase[6 + e : 7 + e] * (s_re[2 + e : 3 + e, at] + s_im[e : e + 1, at])
        )
    return jnp.concatenate(outs, 0)


def match(spec, tiles, info, phase, along):
    along[...] = jnp.zeros_like(along)

    def one(i, carry):
        along[i, 0:2, :] = along_of(spec[i], tiles[...], info[i], phase[i])
        return carry

    lax.fori_loop(0, PAIRS, one, 0, unroll=16)


def weigh(along, info, w_low, w_high, turn):
    flat = info[...].reshape(C * 16, N)
    row = iota((C * 16, 1), 0)
    live = jnp.where((row & 7) < 2, flat[:, 3:4], 0.0)
    score = jnp.sum(along[...].reshape(C * 16, N), 1, keepdims=True) * (1.0 / N)
    weight = (0.5 + 1.0 / (1.0 + jnp.exp(-score))) * live
    high = weight * flat[:, 0:1]
    low = weight - high
    w_low[...] = jnp.broadcast_to(low, (C * 16, N)).reshape(PAIRS, 8, N)
    w_high[...] = jnp.broadcast_to(high, (C * 16, N)).reshape(PAIRS, 8, N)
    lane = iota((C * 16, N), 1)
    at = flat[:, 4:5].astype(I32) + turn * 16
    table = jnp.where(lane == at, score * live, 0.0).reshape(C, 16, N)
    return jnp.sum(table, 1), jnp.sum(low, 0, keepdims=True), jnp.sum(high, 0, keepdims=True)


def weighted(moved, w_low, w_high, low, high):
    def one(i, carry):
        low, high = carry
        wl, wh = w_low[i], w_high[i]
        for e in range(2):
            patch = moved[2 * i + e].astype(F32)
            low = low + patch * wl[e : e + 1]
            high = high + patch * wh[e : e + 1]
        return low, high

    return lax.fori_loop(0, PAIRS, one, (low, high), unroll=16)


def first_kernel(got, tiles, right, left, rows, msg, spec, moved, phase, info, table, along, w_low, w_high):
    flat = got[:, CAP * N :, :].astype(F32).reshape(C * 16, N)
    row, lane = iota((C * 16, N), 0), iota((C * 16, N), 1)
    info[...] = flat.reshape(PAIRS, 8, N)
    amount = jnp.where((row[:, 0:1] & 7) < 4, flat[:, 1:2], flat[:, 2:3]).astype(I32) & (N - 1)
    wave = dot((lane == amount).astype(BF16), rows[...])
    phase[...] = jnp.where((row & 3) < 2, wave[:, :N], wave[:, N:]).reshape(PAIRS, 8, N)

    def one(i, carry):
        at = pl.multiple_of((i % 2) * 2 * N, 2 * N)
        pair = got[i // 2, pl.ds(at, 2 * N), :]
        both = transform_pair(pair, right[...], left[...])
        spec[i] = both
        text = info[i]
        for e in range(2):
            down = (-text[e, 1].astype(I32)) & (N - 1)
            across = (-text[e, 2].astype(I32)) & (N - 1)
            patch = pltpu.roll(pair[e * N : (e + 1) * N].astype(F32), down, 0)
            moved[2 * i + e] = pltpu.roll(patch, across, 1).astype(BF16)
        return carry

    lax.fori_loop(0, PAIRS, one, 0, unroll=16)
    match(spec, tiles, info, phase, along)
    scores, low_sum, high_sum = weigh(along, info, w_low, w_high, 0)
    table[...] = scores
    zero = jnp.zeros((N, N), F32)
    low, high = weighted(moved, w_low, w_high, zero, zero)
    lines = [jnp.broadcast_to(v, (1, N)) for s in (low_sum, high_sum) for v in pieces(s)]
    tail = jnp.concatenate(lines + [jnp.zeros((2, N), F32)], 0).astype(BF16)
    low, high = low.astype(BF16), high.astype(BF16)
    for b in range(C):
        msg[b, :N, :] = low
        msg[b, N : 2 * N, :] = high
        msg[b, 2 * N :, :] = tail


def second_kernel(got, old, spec, moved, phase, info, table, right, left, msg, tables_out, along, w_low, w_high, tiles):
    total = jnp.zeros((2 * N, N), F32)
    tail = jnp.zeros((8, N), F32)
    for b in range(C):
        total = total + got[b, : 2 * N, :].astype(F32)
        tail = tail + got[b, 2 * N :, :].astype(F32)
    fresh = []
    for p in range(PD):
        count = tail[3 * p : 3 * p + 1] + tail[3 * p + 1 : 3 * p + 2] + tail[3 * p + 2 : 3 * p + 3]
        part = old[p * N : (p + 1) * N, :].astype(F32) + total[p * N : (p + 1) * N]
        fresh.append((part / (1.0 + count)).astype(BF16))
    tiles[...] = transform_pair(jnp.concatenate(fresh, 0), right[...], left[...])
    match(spec, tiles, info, phase, along)
    scores, low_sum, high_sum = weigh(along, info, w_low, w_high, 1)
    tables_out[...] = table[...] + scores
    own = jnp.where(place()[0] == 0, 1.0, 0.0)
    low, high = weighted(
        moved, w_low, w_high, fresh[0].astype(F32) * own, fresh[1].astype(F32) * own
    )
    lines = [
        jnp.broadcast_to(v, (1, N)) for s in (low_sum, high_sum) for v in pieces(s + own)
    ]
    tail = jnp.concatenate(lines + [jnp.zeros((2, N), F32)], 0).astype(BF16)
    low, high = low.astype(BF16), high.astype(BF16)
    msg[...] = jnp.zeros_like(msg)
    half = own_half()
    for b in range(C):
        msg[half + b, :SLAB, :] = low[b * SLAB : (b + 1) * SLAB]
        msg[half + b, SLAB : 2 * SLAB, :] = high[b * SLAB : (b + 1) * SLAB]
        msg[half + b, 2 * SLAB :, :] = tail


def finish_kernel(got, table, msg):
    half = own_half()
    total = got[half].astype(F32)
    for b in range(1, C):
        total = total + got[half + b].astype(F32)
    tail = total[2 * SLAB :]
    slab = []
    for p in range(PD):
        count = tail[3 * p : 3 * p + 1] + tail[3 * p + 1 : 3 * p + 2] + tail[3 * p + 2 : 3 * p + 3]
        slab.append(total[p * SLAB : (p + 1) * SLAB] / count)
    slab = jnp.concatenate(slab, 0).astype(BF16)
    parts = pieces(table[...])
    pad = jnp.zeros((5, N), F32)
    for v in range(C):
        lines = jnp.concatenate([part[v : v + 1] for part in parts] + [pad], 0).astype(BF16)
        for y in range(C):
            msg[y * C + v, : 2 * SLAB, :] = slab
            msg[y * C + v, 2 * SLAB :, :] = lines


def place_kernel(got, out, scores, sems):
    y, _, q = place()
    copies = []
    for z in range(C):
        group = (z - q) & (C - 1)
        for p in range(PD):
            copies.append(
                pltpu.make_async_copy(
                    got.at[:, z, p * SLAB : (p + 1) * SLAB, :],
                    out.at[PD * group + p],
                    sems.at[PD * z + p],
                )
            )
    for copy in copies:
        copy.start()
    total = jnp.zeros((8, N), F32)
    for c in range(C):
        total = total + got[y, c, 2 * SLAB :, :].astype(F32)
    line = total[0:1] + total[1:2] + total[2:3]
    for j in range(2 * PD):
        scores[j // PD, 0, j % PD, :, :] = line[:, j * C : (j + 1) * C]
    for copy in copies:
        copy.wait()


def call(kernel, outs, ins, scratch, args, flops=1e8, grant=16, spread=None):
    spaces = {"s": pltpu.SMEM, "v": pltpu.VMEM, "h": pltpu.HBM}
    size = sum(int(np.prod(o.shape)) * o.dtype.itemsize for o in outs)
    return pl.pallas_call(
        kernel,
        out_shape=outs,
        in_specs=[pl.BlockSpec(memory_space=spaces[i]) for i in ins],
        out_specs=[pl.BlockSpec(memory_space=spaces[o]) for o in spread or "v" * len(outs)],
        scratch_shapes=scratch,
        compiler_params=pltpu.CompilerParams(vmem_limit_bytes=grant << 20),
        cost_estimate=pl.CostEstimate(
            flops=int(flops), bytes_accessed=size + (1 << 20), transcendentals=0
        ),
    )(*args)


def struct(shape, dtype):
    return jax.ShapeDtypeStruct(shape, dtype)


def number(y, z, q):
    return (y * C + z) * C + q


def along_z():
    return [[y * C + z for z in range(C)] for y in range(C)]


def along_y():
    return [[y * C + z for y in range(C)] for z in range(C)]


def across():
    groups = []
    for z in range(C):
        pairs = [(a, (z - a) % C) for a in range(C) if a < (z - a) % C]
        if z % 2 == 0:
            pairs.append((z // 2, z // 2 + C // 2))
        for pair in pairs:
            groups.append([number(y, z, q) for q in pair for y in range(C)])
    return groups


def exchange(value, axis, groups=None):
    return lax.all_to_all(
        value, axis, split_axis=0, concat_axis=0, axis_index_groups=groups, tiled=True
    )


def local(frames, offsets, assign, residual, template):
    right, left, rows = (jnp.asarray(t) for t in tables())
    off = offsets.reshape(PD, 2)
    asg = assign.reshape(PD, C)
    res = residual.reshape(PD, C, 2).transpose(0, 2, 1)
    _, z, q = place()
    other = (z - q) & (C - 1)
    small = (PAIRS, 8, N)
    (dealt,) = call(
        deal_kernel,
        [struct((C, ROWS, N), BF16)],
        "hhhh",
        [
            pltpu.VMEM((PD, N, C * N), BF16),
            pltpu.SMEM((PD, 2), I32),
            pltpu.SMEM((PD, C), I32),
            pltpu.SMEM((PD, 2, C), I32),
            pltpu.VMEM((PD, N, C * N), BF16),
            pltpu.VMEM((C * CAP // 2, 8, N), F32),
            pltpu.SMEM((C,), I32),
            pltpu.SemaphoreType.DMA((4,)),
        ],
        (off, asg, res, frames[0]),
        grant=63,
    )
    got = exchange(dealt, "tm", along_z())
    swap = [
        (number(a, b, c), number(a, b, (b - c) % C))
        for a in range(C)
        for b in range(C)
        for c in range(C)
    ]
    mine = lax.dynamic_slice_in_dim(template, PD * other, PD, 0).reshape(PD * N, N)
    old = lax.ppermute(mine, ("tm", "plane"), swap)
    (tiles,) = call(tile_kernel, [struct((2 * N, 2 * N), F32)], "vvv", [], (old, right, left))
    scratch = [pltpu.VMEM(small, F32) for _ in range(3)]
    msg, spec, moved, phase, info, table = call(
        first_kernel,
        [
            struct((C, 2 * N + 8, N), BF16),
            struct((PAIRS, 2 * N, 2 * N), F32),
            struct((2 * PAIRS, N, N), BF16),
            struct(small, F32),
            struct(small, F32),
            struct((C, N), F32),
        ],
        "vvvvv",
        scratch,
        (got, tiles, right, left, rows),
        flops=1e9,
    )
    got = exchange(msg, "tm", along_y())
    msg, table = call(
        second_kernel,
        [struct((2 * C, 2 * SLAB + 8, N), BF16), struct((C, N), F32)],
        "vvvvvvvvv",
        scratch + [pltpu.VMEM((2 * N, 2 * N), F32)],
        (got, old, spec, moved, phase, info, table, right, left),
        flops=1e9,
    )
    got = exchange(msg, ("tm", "plane"), across())
    (msg,) = call(finish_kernel, [struct((C * C, 2 * SLAB + 8, N), BF16)], "vv", [], (got, table))
    got = exchange(msg, "tm")
    out, scores = call(
        place_kernel,
        [struct((PD * C, C, SLAB, N), BF16), struct((2, 1, PD, 1, C), F32)],
        "v",
        [pltpu.SemaphoreType.DMA((PD * C,))],
        (got.reshape(C, C, 2 * SLAB + 8, N),),
        spread="hv",
    )
    return out.reshape(PD * C, N, N), scores


def solution(mesh):
    return jax.shard_map(
        local,
        mesh=mesh,
        in_specs=(
            P("tm", "plane", None, None),
            P("tm", "plane", None),
            P("tm", "plane", None, None, None),
            P("tm", "plane", None, None, None),
            P(None, None, "plane"),
        ),
        out_specs=(P(None, None, "plane"), P(None, "tm", "plane", None, None)),
        check_vma=False,
    )
```
